128 devices in a mesh: shot: 32 (over z, y, core), tm: 4 (over x).
Axes of the slice: x: 4, y: 4, z: 4, core: 2. Of those that a mesh axis runs over, the one named last changes fastest.
Arguments:
- signals: bfloat16 [256, 128, 2048], P('tm', 'shot'), may hold values from -0.59765625 to 0.59765625
- aperture: int32 [128, 128, 128], P('shot'), may hold values from 0 to 2047
- counts: int32 [128, 128], P('shot'), may hold values from 97 to 128, as said below
Outputs:
- prediction: float32 [256, 128, 128], P('tm', None, 'shot')
The draws below stay inside these ranges and needn't reach their ends.
Inputs may be any that keep to these rules, and one draw needn't show every extreme that they name: Slots j >= counts[r, s] of aperture[r, s] are padding and do not enter the prediction. `counts`: in every draw some output trace uses all 128 slots.
All inputs are finite; a program needn't handle non-finite values.
Results may differ from the reference program's by a relative error of at most 0.0003.
Values may be sent and summed in bfloat16 or wider, within the bound.
No kernel may reach another device: no remote copies, remote signals or barrier semaphores. Data moves between devices by JAX's collectives and lax.ppermute only.
A program may use at most 128 MiB of HBM per device.

```python
import jax
import jax.numpy as jnp
from jax import lax

NT = 256
NREC = 2048
AP = 128
SHOTS = 128


def draw_counts(key, part):
    key_count, key_row, key_col = jax.random.split(key, 3)
    raw_draw = jax.random.randint(key_count, (SHOTS, SHOTS), 0, 1 << 20)
    drawn = AP - raw_draw % (AP // 4)
    row_pick = jax.random.randint(key_row, (), 0, SHOTS)
    col_pick = jax.random.randint(key_col, (), 0, SHOTS)
    return drawn.at[row_pick, col_pick].set(AP).astype(jnp.int32)


def touch_ends(values, own_key, least, largest):
    longest = values.shape.index(max(values.shape))
    spots = []
    for shift in (0, 1):
        where = [jax.random.randint(jax.random.fold_in(own_key, axis), (), 0, length) for axis, length in enumerate(values.shape)]
        where[longest] = (where[longest] + shift) % values.shape[longest]
        spots.append(tuple(where))
    return values.at[spots[0]].set(least).at[spots[1]].set(largest)


def block_levels(own_key, extent, shards, least, top_value):
    def one(dim, blocks):
        heights = jax.random.uniform(jax.random.fold_in(jax.random.fold_in(own_key, 6), dim), (blocks,), jnp.float32, least / len(shards), top_value / len(shards))
        return jnp.repeat(jnp.exp(heights), extent[dim] // blocks).reshape((-1,) + (1,) * (len(extent) - dim - 1))

    factor_of = one(*shards[0])
    for cut in shards[1:]:
        factor_of = factor_of * one(*cut)
    return factor_of


def bell_draw(stream_key, dims, scale, reach, cuts=(), kind=jnp.bfloat16):
    array = jax.random.normal(stream_key, dims, jnp.float32) * scale
    if len(cuts) > 0:
        array = block_levels(stream_key, dims, cuts, -0.22, 0.18) * array
    return jnp.clip(array, min=-reach, max=reach).astype(kind)


def setup_inputs(seed: int = 0) -> dict:
    splits = jax.random.split(jax.random.key(seed), 4)
    signals = bell_draw(splits[0], (NT, SHOTS, NREC), 0.1, 0.59765625, ((0, 4), (1, 32)))
    aperture = touch_ends(jax.random.randint(splits[1], (SHOTS, SHOTS, AP), 0, NREC), jax.random.fold_in(splits[1], 1), 0, NREC - 1).astype(jnp.int32)
    counts = draw_counts(jax.random.fold_in(splits[3], 71), 0)
    return {"signals": signals, "aperture": aperture, "counts": counts}


def reference(signals, aperture, counts):
    signal_f32 = signals.astype(jnp.float32)

    def one_receiver(receiver):
        row_lists = aperture[receiver]
        live_mask = jnp.arange(AP, dtype=jnp.int32)[None, :] < counts[receiver][:, None]
        first_side = jnp.take_along_axis(signal_f32, row_lists[None, :, :], axis=2)
        own_traces = lax.dynamic_index_in_dim(signal_f32, receiver, 1, keepdims=False)
        second_side = jnp.take(own_traces, row_lists, axis=1)
        second_side = jnp.where(live_mask[None, :, :], second_side, jnp.zeros_like(second_side))
        spec_first = jnp.fft.rfft(first_side, n=2 * NT, axis=0)
        spec_second = jnp.fft.rfft(second_side, n=2 * NT, axis=0)
        summed = jnp.sum(spec_first * spec_second, axis=2)
        return jnp.fft.irfft(summed, n=2 * NT, axis=0)[:NT]

    stacked = lax.map(one_receiver, jnp.arange(SHOTS, dtype=jnp.int32))
    return jnp.transpose(stacked, (1, 2, 0))
```

```python
import functools
import itertools

import jax
import jax.numpy as jnp
import numpy as np
from jax import lax
from jax.experimental import pallas as pl
from jax.experimental.pallas import tpu as pltpu
from jax.sharding import Mesh
from jax.sharding import PartitionSpec as P

AXES = ("z", "y", "c", "x")
SIZES = (4, 4, 2, 4)
LANES = 128
NT_DIMS = (((1,), (1,)), ((), ()))

PLANE_HOPS = (
    ((0, 1), (0, 1), (0, 0)),
    ((0, 3), (0, 3), (0, 0)),
    ((1, 0), (1, 0), (0, 0)),
    ((3, 0), (3, 0), (0, 0)),
    ((1, 1), (0, 1), (1, 0)),
    ((3, 3), (0, 3), (3, 0)),
    ((1, 3), (1, 0), (0, 3)),
    ((3, 1), (3, 0), (0, 1)),
    ((0, 2), (0, 1), (0, 1)),
    ((3, 2), (0, 3), (3, 3)),
    ((2, 0), (1, 0), (1, 0)),
    ((2, 1), (3, 0), (3, 1)),
    ((1, 2), (0, 1), (1, 1)),
    ((2, 3), (1, 0), (1, 3)),
    ((2, 2), (3, 0), (3, 2)),
)
S_OFFSETS = ((0, 0),) + tuple(hop[0] for hop in PLANE_HOPS)
R_OFFSETS = ((0, 0), (1, 0), (0, 1), (1, 1), (0, 3), (1, 3), (0, 2), (1, 2))


def from_offset(value, dz=0, dy=0, dc=0, dx=0):
    pairs = []
    for place in itertools.product(*(range(n) for n in SIZES)):
        source = tuple((p + d) % n for p, d, n in zip(place, (dz, dy, dc, dx), SIZES))
        pairs.append((int(np.ravel_multi_index(source, SIZES)), int(np.ravel_multi_index(place, SIZES))))
    return lax.ppermute(value, AXES, pairs)


def row_tables():
    list_rows, made_rows = [], []
    for z, y, c, x in itertools.product(*(range(n) for n in SIZES)):
        r_slot = [other * 4 + (x + dx) % 4 for other, dx in R_OFFSETS]
        s_slot = [(z + dz) % 4 * 4 + (y + dy) % 4 for dz, dy in S_OFFSETS]
        list_rows.append([r * 16 + s for r in r_slot for s in s_slot])
        made_rows.append(
            [
                r_slot.index((core ^ c) * 4 + r) * 16 + s_slot.index(s)
                for core in range(2)
                for r in range(4)
                for s in range(16)
            ]
        )
    return np.asarray(list_rows, np.int32), np.asarray(made_rows, np.int32)


def count_kernel(list_ref, out_ref):
    stations = list_ref[0]
    high = stations >> 7
    low = stations & (LANES - 1)
    chunk = lax.broadcasted_iota(jnp.int32, (16, LANES), 0)
    lane = lax.broadcasted_iota(jnp.int32, (LANES, LANES), 0)
    for s in range(stations.shape[0]):
        is_high = (high[s : s + 1, :] == chunk).astype(jnp.float32).astype(jnp.bfloat16)
        is_low = (low[s : s + 1, :] == lane).astype(jnp.float32).astype(jnp.bfloat16)
        out_ref[0, s] = lax.dot_general(is_high, is_low, NT_DIMS, preferred_element_type=jnp.float32)


def station_counts(lists):
    count_r, count_s, _ = lists.shape
    return pl.pallas_call(
        count_kernel,
        grid=(count_r,),
        in_specs=[pl.BlockSpec((1, count_s, LANES), lambda i: (i, 0, 0))],
        out_specs=pl.BlockSpec((1, count_s, 16, LANES), lambda i: (i, 0, 0, 0)),
        out_shape=jax.ShapeDtypeStruct((count_r, count_s, 16, LANES), jnp.float32),
        cost_estimate=pl.CostEstimate(flops=10**9, bytes_accessed=2**20, transcendentals=0),
        name="station_counts",
    )(lists)


def antidiagonals(outer):
    tau = lax.broadcasted_iota(jnp.int32, (LANES, LANES), 0)
    lane = lax.broadcasted_iota(jnp.int32, (LANES, LANES), 1)
    keep = lane >= tau
    near = pltpu.roll(outer[:LANES, :LANES], 0, 1, stride=1, stride_axis=0)
    far = outer[:LANES, LANES:] + outer[LANES:, :LANES]
    far = pltpu.roll(far, 0, 1, stride=1, stride_axis=0)
    first = jnp.sum(jnp.where(keep, near, 0.0), axis=0, keepdims=True)
    second = jnp.sum(jnp.where(keep, far, near), axis=0, keepdims=True)
    return first, second


def pair_kernel(count_s, first_r, first_s, flag_ref, times_ref, r_ref, *refs):
    s_refs = refs[:count_s]
    out_ref, scaled, outer = refs[count_s:]
    length = r_ref.shape[1]
    chunks = r_ref.shape[2] // LANES
    r = pl.program_id(0)
    for s in range(count_s):
        for c in range(chunks):
            cols = slice(c * LANES, (c + 1) * LANES)
            times = jnp.broadcast_to(times_ref[0, s, c : c + 1, :], (16, LANES)).astype(jnp.bfloat16)
            times = jnp.concatenate([times] * (length // 16), axis=0)
            scaled[s * length : (s + 1) * length, cols] = s_refs[s][:, cols] * times
    outer[...] = lax.dot_general(scaled[...], r_ref[0], NT_DIMS, preferred_element_type=jnp.float32)
    for s in range(count_s):
        rows = slice(s * length, (s + 1) * length)

        @pl.when(flag_ref[first_r + r, first_s + s] != 0)
        def _():
            for c in range(chunks):
                cols = slice(c * LANES, (c + 1) * LANES)
                times = jnp.broadcast_to(times_ref[0, s, c : c + 1, :], (length, LANES))
                whole = s_refs[s][:, cols].astype(jnp.float32) * times
                scaled[rows, cols] = (whole - scaled[rows, cols].astype(jnp.float32)).astype(jnp.bfloat16)
            outer[rows, :] += lax.dot_general(
                scaled[rows, :], r_ref[0], NT_DIMS, preferred_element_type=jnp.float32
            )

        first, second = antidiagonals(outer[rows, :])
        out_ref[0, s, 0:1, :] = first
        out_ref[0, s, 1:2, :] = second


def predict(flags, times, r_shots, s_shots, first_r, first_s):
    count_r, length, stations = r_shots.shape
    count_s = len(s_shots)
    grid_spec = pltpu.PrefetchScalarGridSpec(
        num_scalar_prefetch=1,
        grid=(count_r,),
        in_specs=[
            pl.BlockSpec(
                (1, count_s, 16, LANES), lambda i, f: (first_r + i, first_s // count_s, 0, 0)
            ),
            pl.BlockSpec((1, length, stations), lambda i, f: (i, 0, 0)),
        ]
        + [pl.BlockSpec((length, stations), lambda i, f: (0, 0))] * count_s,
        out_specs=pl.BlockSpec((1, count_s, 2, LANES), lambda i, f: (i, 0, 0, 0)),
        scratch_shapes=[
            pltpu.VMEM((count_s * length, stations), jnp.bfloat16),
            pltpu.VMEM((count_s * length, length), jnp.float32),
        ],
    )
    return pl.pallas_call(
        functools.partial(pair_kernel, count_s, first_r, first_s),
        grid_spec=grid_spec,
        out_shape=jax.ShapeDtypeStruct((count_r, count_s, 2, LANES), jnp.float32),
        compiler_params=pltpu.CompilerParams(vmem_limit_bytes=48 << 20),
        cost_estimate=pl.CostEstimate(
            flops=count_r * count_s * 2 * length * length * stations * 2,
            bytes_accessed=(count_r + count_s) * length * stations * 2,
            transcendentals=0,
        ),
        name="pairs",
    )(flags, times, r_shots, *s_shots)


def body(signals, aperture, counts):
    length_win, group, stations = signals.shape
    shots = aperture.shape[1]
    slots = aperture.shape[2]
    z, y, c, x = (lax.axis_index(name) for name in AXES)

    own = lax.all_to_all(jnp.transpose(signals, (1, 0, 2)), "x", 0, 0, tiled=True)
    own = own.reshape(4 * length_win, stations)

    live = jnp.arange(slots, dtype=jnp.int32) < counts[:, :, None]
    lists = jnp.where(live, aperture, -1).reshape(group, 16, 2, 4, slots)
    lists = lax.dynamic_index_in_dim(lists, x, 3, keepdims=False)
    mine = lax.dynamic_index_in_dim(lists, c, 2, keepdims=False)
    theirs = from_offset(lax.dynamic_index_in_dim(lists, 1 - c, 2, keepdims=False), dc=1)
    lists = jnp.stack([mine, theirs]).reshape(2 * group * 16, slots)
    list_rows, made_rows = row_tables()
    device = ((z * 4 + y) * 2 + c) * 4 + x
    rows = lax.dynamic_index_in_dim(jnp.asarray(list_rows), device, 0, keepdims=False)
    lists = jnp.take(lists, rows, axis=0).reshape(len(R_OFFSETS), 16, slots)
    times = station_counts(lists)
    whole = times.astype(jnp.int32)
    flags = jnp.max(whole & (whole - 1), axis=(2, 3))

    held = {(0, 0): own}
    lines = {0: own, 1: from_offset(own, dx=1), 3: from_offset(own, dx=3)}
    for offset, (dz, dy), forwarded in PLANE_HOPS:
        held[offset] = from_offset(held[forwarded], dz=dz, dy=dy)
        if offset == (3, 0):
            lines[2] = from_offset(lines[1], dx=1)
    r_shots = []
    for other, dx in R_OFFSETS:
        r_shots.append(from_offset(lines[dx], dc=1) if other else lines[dx])
    near = jnp.stack(r_shots[:6])
    away = jnp.stack(r_shots[6:])

    blocks = []
    for first_s in range(0, 16, 4):
        s_shots = [held[offset] for offset in S_OFFSETS[first_s : first_s + 4]]
        blocks.append(
            jnp.concatenate(
                [predict(flags, times, near, s_shots, 0, first_s), predict(flags, times, away, s_shots, 6, first_s)]
            )
        )
    made = jnp.concatenate(blocks, axis=1).reshape(len(R_OFFSETS) * 16, 4 * length_win)

    rows = lax.dynamic_index_in_dim(jnp.asarray(made_rows), device, 0, keepdims=False)
    made = jnp.take(made, rows, axis=0).reshape(2, group, 16, 4, length_win)
    made = jnp.transpose(made, (0, 3, 4, 1, 2)).reshape(8, length_win, group, 16)
    made = lax.all_to_all(made, ("c", "x"), 0, 0, tiled=True)
    made = made.reshape(2, 4, length_win, group, 16)
    return jnp.transpose(made, (2, 4, 0, 1, 3)).reshape(length_win, shots, group)


def solution(mesh):
    fine = Mesh(np.asarray(mesh.devices).reshape(SIZES), AXES)
    shot = ("z", "y", "c")
    in_specs = (P("x", shot, None), P(shot, None, None), P(shot, None))
    return jax.shard_map(body, mesh=fine, in_specs=in_specs, out_specs=P("x", None, shot), check_vma=False)
```

```python
import functools
import itertools

import jax
import jax.numpy as jnp
import numpy as np
from jax import lax
from jax.experimental import pallas as pl
from jax.experimental.pallas import tpu as pltpu
from jax.sharding import Mesh
from jax.sharding import PartitionSpec as P

AXES = ("z", "y", "c", "x")
SIZES = (4, 4, 2, 4)
LANES = 128
NT_DIMS = (((1,), (1,)), ((), ()))

ROUNDS = (
    (((0, 1), (0, 1), (0, 0)), ((0, 3), (0, 3), (0, 0)), ((1, 0), (1, 0), (0, 0))),
    (((3, 0), (3, 0), (0, 0)), ((1, 1), (0, 1), (1, 0)), ((1, 3), (0, 3), (1, 0)), ((2, 0), (1, 0), (1, 0))),
    (((0, 2), (0, 1), (0, 1)), ((3, 3), (0, 3), (3, 0)), ((2, 1), (1, 0), (1, 1)), ((3, 1), (3, 0), (0, 1))),
    (((2, 2), (0, 1), (2, 1)), ((1, 2), (1, 0), (0, 2)), ((2, 3), (0, 3), (2, 0)), ((3, 2), (3, 0), (0, 2))),
)
S_OFFSETS = ((0, 0),) + tuple(hop[0] for hops in ROUNDS for hop in hops)
R_OFFSETS = ((0, 0), (0, 1), (0, 3), (1, 0), (1, 1), (1, 3), (0, 2), (1, 2))


def from_offset(value, dz=0, dy=0, dc=0, dx=0):
    pairs = []
    for place in itertools.product(*(range(n) for n in SIZES)):
        source = tuple((p + d) % n for p, d, n in zip(place, (dz, dy, dc, dx), SIZES))
        pairs.append((int(np.ravel_multi_index(source, SIZES)), int(np.ravel_multi_index(place, SIZES))))
    return lax.ppermute(value, AXES, pairs)


def row_tables():
    list_rows, made_rows = [], []
    for z, y, c, x in itertools.product(*(range(n) for n in SIZES)):
        r_slot = [other * 4 + (x + dx) % 4 for other, dx in R_OFFSETS]
        s_slot = [(z + dz) % 4 * 4 + (y + dy) % 4 for dz, dy in S_OFFSETS]
        list_rows.append([r * 16 + s for r in r_slot for s in s_slot])
        made_rows.append(
            [
                r_slot.index((core ^ c) * 4 + r) * 16 + s_slot.index(s)
                for core in range(2)
                for r in range(4)
                for s in range(16)
            ]
        )
    return np.asarray(list_rows, np.int32), np.asarray(made_rows, np.int32)


def count_kernel(list_ref, out_ref):
    stations = list_ref[0]
    high = stations >> 7
    low = stations & (LANES - 1)
    chunk = lax.broadcasted_iota(jnp.int32, (16, LANES), 0)
    lane = lax.broadcasted_iota(jnp.int32, (LANES, LANES), 0)
    for s in range(stations.shape[0]):
        is_high = (high[s : s + 1, :] == chunk).astype(jnp.float32).astype(jnp.bfloat16)
        is_low = (low[s : s + 1, :] == lane).astype(jnp.float32).astype(jnp.bfloat16)
        out_ref[0, s] = lax.dot_general(is_high, is_low, NT_DIMS, preferred_element_type=jnp.float32)


def station_counts(lists):
    count_r, count_s, _ = lists.shape
    return pl.pallas_call(
        count_kernel,
        grid=(count_r,),
        in_specs=[pl.BlockSpec((1, count_s, LANES), lambda i: (i, 0, 0))],
        out_specs=pl.BlockSpec((1, count_s, 16, LANES), lambda i: (i, 0, 0, 0)),
        out_shape=jax.ShapeDtypeStruct((count_r, count_s, 16, LANES), jnp.float32),
        cost_estimate=pl.CostEstimate(flops=10**9, bytes_accessed=2**20, transcendentals=0),
        name="station_counts",
    )(lists)


def antidiagonals(outer):
    tau = lax.broadcasted_iota(jnp.int32, (LANES, LANES), 0)
    lane = lax.broadcasted_iota(jnp.int32, (LANES, LANES), 1)
    keep = lane >= tau
    near = pltpu.roll(outer[:LANES, :LANES], 0, 1, stride=1, stride_axis=0)
    far = outer[:LANES, LANES:] + outer[LANES:, :LANES]
    far = pltpu.roll(far, 0, 1, stride=1, stride_axis=0)
    first = jnp.sum(jnp.where(keep, near, 0.0), axis=0, keepdims=True)
    second = jnp.sum(jnp.where(keep, far, near), axis=0, keepdims=True)
    return first, second


def pair_kernel(r_parts, count_s, first_r, first_s, flag_ref, times_ref, *refs):
    count_arrays = 1 + max(array for array, _ in r_parts)
    r_refs = refs[:count_arrays]
    s_refs = refs[count_arrays : count_arrays + count_s]
    out_ref, scaled, outer, r_buf, sems = refs[count_arrays + count_s :]
    length, stations = s_refs[0].shape
    chunks = stations // LANES
    r = pl.program_id(0)
    slot = lax.rem(r, 2)

    def fetch(part):
        array, row = r_parts[part]
        source = r_refs[array] if row is None else r_refs[array].at[row]
        return pltpu.make_async_copy(source, r_buf.at[part % 2], sems.at[part % 2])

    @pl.when(r == 0)
    def _():
        fetch(0).start()

    for part in range(1, len(r_parts)):

        @pl.when(r == part - 1)
        def _():
            fetch(part).start()

    for s in range(count_s):
        for c in range(chunks):
            cols = slice(c * LANES, (c + 1) * LANES)
            times = jnp.broadcast_to(times_ref[0, s, c : c + 1, :], (16, LANES)).astype(jnp.bfloat16)
            times = jnp.concatenate([times] * (length // 16), axis=0)
            scaled[s * length : (s + 1) * length, cols] = s_refs[s][:, cols] * times
    pltpu.make_async_copy(r_buf.at[slot], r_buf.at[slot], sems.at[slot]).wait()
    outer[...] = lax.dot_general(scaled[...], r_buf[slot], NT_DIMS, preferred_element_type=jnp.float32)
    for s in range(count_s):
        rows = slice(s * length, (s + 1) * length)
        flag = flag_ref[first_r + r, first_s + s]

        @pl.when(flag != 0)
        def _():
            def one(pair, carry):
                @pl.when((flag >> pair) & 1 != 0)
                def _():
                    parts = []
                    for half in range(2):
                        cols = pl.ds(pl.multiple_of(pair * 2 * LANES + half * LANES, LANES), LANES)
                        times = jnp.broadcast_to(times_ref[0, s, pl.ds(pair * 2 + half, 1), :], (length, LANES))
                        whole = s_refs[s][:, cols].astype(jnp.float32) * times
                        parts.append((whole - scaled[rows, cols].astype(jnp.float32)).astype(jnp.bfloat16))
                    both = pl.ds(pl.multiple_of(pair * 2 * LANES, 2 * LANES), 2 * LANES)
                    outer[rows, :] += lax.dot_general(
                        jnp.concatenate(parts, axis=1),
                        r_buf[slot, :, both],
                        NT_DIMS,
                        preferred_element_type=jnp.float32,
                    )

                return carry

            lax.fori_loop(0, chunks // 2, one, 0)

        first, second = antidiagonals(outer[rows, :])
        out_ref[0, s, 0:1, :] = first
        out_ref[0, s, 1:2, :] = second


def predict(flags, times, r_arrays, s_shots, first_r, first_s):
    r_parts = []
    for number, array in enumerate(r_arrays):
        r_parts += [(number, row) for row in range(array.shape[0])] if array.ndim == 3 else [(number, None)]
    count_r, count_s = len(r_parts), len(s_shots)
    length, stations = s_shots[0].shape
    grid_spec = pltpu.PrefetchScalarGridSpec(
        num_scalar_prefetch=1,
        grid=(count_r,),
        in_specs=[
            pl.BlockSpec((1, count_s, 16, LANES), lambda i, f: (first_r + i, first_s // count_s, 0, 0)),
        ]
        + [pl.BlockSpec(memory_space=pl.ANY)] * len(r_arrays)
        + [pl.BlockSpec((length, stations), lambda i, f: (0, 0), pipeline_mode=pl.Buffered(1))] * count_s,
        out_specs=pl.BlockSpec((1, count_s, 2, LANES), lambda i, f: (i, 0, 0, 0)),
        scratch_shapes=[
            pltpu.VMEM((count_s * length, stations), jnp.bfloat16),
            pltpu.VMEM((count_s * length, length), jnp.float32),
            pltpu.VMEM((2, length, stations), jnp.bfloat16),
            pltpu.SemaphoreType.DMA((2,)),
        ],
    )
    return pl.pallas_call(
        functools.partial(pair_kernel, tuple(r_parts), count_s, first_r, first_s),
        grid_spec=grid_spec,
        out_shape=jax.ShapeDtypeStruct((count_r, count_s, 2, LANES), jnp.float32),
        compiler_params=pltpu.CompilerParams(vmem_limit_bytes=32 << 20),
        cost_estimate=pl.CostEstimate(
            flops=count_r * count_s * 2 * length * length * stations * 2,
            bytes_accessed=(count_r + count_s) * length * stations * 2,
            transcendentals=0,
        ),
        name="pairs",
    )(flags, times, *r_arrays, *s_shots)


def body(signals, aperture, counts):
    length_win, group, stations = signals.shape
    shots = aperture.shape[1]
    slots = aperture.shape[2]
    z, y, c, x = (lax.axis_index(name) for name in AXES)

    live = jnp.arange(slots, dtype=jnp.int32) < counts[:, :, None]
    lists = jnp.where(live, aperture, -1).reshape(group, 16, 2, 4, slots)
    lists = lax.dynamic_index_in_dim(lists, x, 3, keepdims=False)
    mine = lax.dynamic_index_in_dim(lists, c, 2, keepdims=False)
    theirs = from_offset(lax.dynamic_index_in_dim(lists, 1 - c, 2, keepdims=False), dc=1)

    native = jnp.transpose(signals, (1, 0, 2))
    windows = [lax.dynamic_index_in_dim(native, x, 0, keepdims=False)]
    for dx in (1, 2, 3):
        windows.append(from_offset(lax.dynamic_index_in_dim(native, (x - dx) % 4, 0, keepdims=False), dx=dx))
    windows = jnp.stack(windows + windows)
    own = lax.dynamic_slice_in_dim(windows, (4 - x) % 4, 4, 0).reshape(4 * length_win, stations)
    own, mine, theirs = lax.optimization_barrier((own, mine, theirs))

    held = {(0, 0): own}

    def travel(number):
        for offset, (dz, dy), forwarded in ROUNDS[number]:
            held[offset] = from_offset(held[forwarded], dz=dz, dy=dy)

    def meet(number, *others):
        names = [hop[0] for hop in ROUNDS[number]]
        values = lax.optimization_barrier([held[name] for name in names] + list(others))
        held.update(zip(names, values))
        return values[len(names) :]

    travel(0)
    right, left = meet(0, from_offset(own, dx=1), from_offset(own, dx=3))

    lists = jnp.stack([mine, theirs]).reshape(2 * group * 16, slots)
    list_rows, made_rows = row_tables()
    device = ((z * 4 + y) * 2 + c) * 4 + x
    rows = lax.dynamic_index_in_dim(jnp.asarray(list_rows), device, 0, keepdims=False)
    lists = jnp.take(lists, rows, axis=0).reshape(len(R_OFFSETS), 16, slots)
    times = station_counts(lists)
    whole = times.astype(jnp.int32).reshape(len(R_OFFSETS), 16, 8, 2 * LANES)
    odd = jnp.max((whole & (whole - 1) != 0).astype(jnp.int32), axis=3)
    flags = jnp.sum(odd << jnp.arange(8, dtype=jnp.int32), axis=2)

    def some(first_s, count=4):
        return [held[offset] for offset in S_OFFSETS[first_s : first_s + count]]

    near = jnp.stack([own, right, left])
    near_other = from_offset(near, dc=1)
    travel(1)
    right, near_other = lax.optimization_barrier((right, near_other))
    away = from_offset(right, dx=1)
    (near_other,) = meet(1, near_other)
    blocks = [predict(flags, times, [near, near_other], some(0), 0, 0)]
    travel(2)
    blocks.append(predict(flags, times, [near, near_other], some(4), 0, 4))
    (away,) = meet(2, away)
    away_other = from_offset(away, dc=1)
    travel(3)
    ends = [predict(flags, times, [away, away_other], some(first_s), 6, first_s) for first_s in (0, 4)]
    for first_s in (8, 12):
        both = predict(flags, times, [near, near_other, away, away_other], some(first_s), 0, first_s)
        blocks.append(both)
    head = jnp.concatenate([jnp.concatenate(blocks[:2], axis=1), jnp.concatenate(ends, axis=1)], axis=0)
    made = jnp.concatenate([head] + blocks[2:], axis=1).reshape(len(R_OFFSETS) * 16, 4 * length_win)

    rows = lax.dynamic_index_in_dim(jnp.asarray(made_rows), device, 0, keepdims=False)
    made = jnp.take(made, rows, axis=0).reshape(2, group, 16, 4, length_win)
    made = jnp.transpose(made, (0, 3, 4, 1, 2)).reshape(8, length_win, group, 16)
    made = lax.all_to_all(made, ("c", "x"), 0, 0, tiled=True)
    made = made.reshape(2, 4, length_win, group, 16)
    return jnp.transpose(made, (2, 4, 0, 1, 3)).reshape(length_win, shots, group)


def solution(mesh):
    fine = Mesh(np.asarray(mesh.devices).reshape(SIZES), AXES)
    shot = ("z", "y", "c")
    in_specs = (P("x", shot, None), P(shot, None, None), P(shot, None))
    return jax.shard_map(body, mesh=fine, in_specs=in_specs, out_specs=P("x", None, shot), check_vma=False)
```

```python
import functools
import itertools

import jax
import jax.numpy as jnp
import numpy as np
from jax import lax
from jax.experimental import pallas as pl
from jax.experimental.pallas import tpu as pltpu
from jax.sharding import Mesh
from jax.sharding import PartitionSpec as P

AXES = ("z", "y", "c", "x")
SIZES = (4, 4, 2, 4)
LANES = 128
NT_DIMS = (((1,), (1,)), ((), ()))

ROUNDS = (
    (((0, 1), (0, 1), (0, 0)), ((0, 3), (0, 3), (0, 0)), ((1, 0), (1, 0), (0, 0)), ((3, 0), (3, 0), (0, 0))),
    (((1, 1), (0, 1), (1, 0)), ((3, 3), (0, 3), (3, 0)), ((1, 3), (1, 0), (0, 3)), ((3, 1), (3, 0), (0, 1))),
    (((0, 2), (0, 1), (0, 1)), ((3, 2), (0, 3), (3, 3)), ((2, 0), (1, 0), (1, 0)), ((2, 1), (3, 0), (3, 1))),
    (((2, 2), (0, 1), (2, 1)), ((1, 2), (0, 3), (1, 3)), ((2, 3), (3, 0), (3, 3))),
)
S_OFFSETS = ((0, 0),) + tuple(hop[0] for hops in ROUNDS for hop in hops)


def from_offset(value, dz=0, dy=0, dc=0, dx=0):
    pairs = []
    for place in itertools.product(*(range(n) for n in SIZES)):
        source = tuple((p + d) % n for p, d, n in zip(place, (dz, dy, dc, dx), SIZES))
        pairs.append((int(np.ravel_multi_index(source, SIZES)), int(np.ravel_multi_index(place, SIZES))))
    return lax.ppermute(value, AXES, pairs)


def row_tables():
    list_rows, made_rows = [], []
    for z, y, c, x in itertools.product(*(range(n) for n in SIZES)):
        s_slot = [(z + dz) % 4 * 4 + (y + dy) % 4 for dz, dy in S_OFFSETS]
        cores = (0, 1) if c == 0 else (1, 0)
        list_rows.append([(core * 4 + r) * 16 + s for core in cores for r in range(4) for s in s_slot])
        made_rows.append([r * 16 + s_slot.index(s) for r in range(8) for s in range(16)])
    return np.asarray(list_rows, np.int32), np.asarray(made_rows, np.int32)


def count_kernel(list_ref, out_ref):
    stations = list_ref[0]
    high = stations >> 7
    low = stations & (LANES - 1)
    chunk = lax.broadcasted_iota(jnp.int32, (16, LANES), 0)
    lane = lax.broadcasted_iota(jnp.int32, (LANES, LANES), 0)
    for s in range(stations.shape[0]):
        is_high = (high[s : s + 1, :] == chunk).astype(jnp.float32).astype(jnp.bfloat16)
        is_low = (low[s : s + 1, :] == lane).astype(jnp.float32).astype(jnp.bfloat16)
        out_ref[0, s] = lax.dot_general(is_high, is_low, NT_DIMS, preferred_element_type=jnp.float32)


def station_counts(lists):
    count_r, count_s, _ = lists.shape
    return pl.pallas_call(
        count_kernel,
        grid=(count_r,),
        in_specs=[pl.BlockSpec((1, count_s, LANES), lambda i: (i, 0, 0))],
        out_specs=pl.BlockSpec((1, count_s, 16, LANES), lambda i: (i, 0, 0, 0)),
        out_shape=jax.ShapeDtypeStruct((count_r, count_s, 16, LANES), jnp.float32),
        cost_estimate=pl.CostEstimate(flops=10**9, bytes_accessed=2**20, transcendentals=0),
        name="station_counts",
    )(lists)


def antidiagonals(outer):
    tau = lax.broadcasted_iota(jnp.int32, (LANES, LANES), 0)
    lane = lax.broadcasted_iota(jnp.int32, (LANES, LANES), 1)
    keep = lane >= tau
    near = pltpu.roll(outer[:LANES, :LANES], 0, 1, stride=1, stride_axis=0)
    far = outer[:LANES, LANES:] + outer[LANES:, :LANES]
    far = pltpu.roll(far, 0, 1, stride=1, stride_axis=0)
    first = jnp.sum(jnp.where(keep, near, 0.0), axis=0, keepdims=True)
    second = jnp.sum(jnp.where(keep, far, near), axis=0, keepdims=True)
    return first, second


def pair_kernel(first_s, count_s, flag_ref, times_ref, r_ref, *refs):
    s_refs = refs[:count_s]
    out_ref, scaled, outer, rest, r_buf, sems = refs[count_s:]
    length, stations = s_refs[0].shape
    _, windows, group, window_len, _ = r_ref.shape
    chunks = stations // LANES
    r = pl.program_id(0)
    slot = lax.rem(r, 2)

    def fetches(number, to):
        for w in range(windows):
            yield pltpu.make_async_copy(
                r_ref.at[number // group, w, lax.rem(number, group)],
                r_buf.at[to, pl.ds(w * window_len, window_len)],
                sems.at[to, w],
            )

    @pl.when(r == 0)
    def _():
        for fetch in fetches(r, 0):
            fetch.start()

    @pl.when(r + 1 < pl.num_programs(0))
    def _():
        for fetch in fetches(r + 1, 1 - slot):
            fetch.start()

    for fetch in fetches(r, slot):
        fetch.wait()

    for s in range(count_s):
        for c in range(chunks):
            cols = slice(c * LANES, (c + 1) * LANES)
            times = jnp.broadcast_to(times_ref[0, first_s + s, c : c + 1, :], (16, LANES)).astype(jnp.bfloat16)
            times = jnp.concatenate([times] * (length // 16), axis=0)
            scaled[s * length : (s + 1) * length, cols] = s_refs[s][:, cols] * times
    outer[...] = lax.dot_general(scaled[...], r_buf[slot], NT_DIMS, preferred_element_type=jnp.float32)
    for s in range(count_s):
        first, second = antidiagonals(outer[s * length : (s + 1) * length, :])
        out_ref[0, s, 0:1, :] = first
        out_ref[0, s, 1:2, :] = second

    for s in range(count_s):
        rows = slice(s * length, (s + 1) * length)
        flag = flag_ref[r, first_s + s]

        @pl.when(flag != 0)
        def _():
            rest[...] = jnp.zeros_like(rest)

            def one(pair, carry):
                @pl.when((flag >> pair) & 1 != 0)
                def _():
                    parts = []
                    for half in range(2):
                        cols = pl.ds(pl.multiple_of((pair * 2 + half) * LANES, LANES), LANES)
                        times = times_ref[0, first_s + s, pl.ds(pair * 2 + half, 1), :]
                        whole = s_refs[s][:, cols].astype(jnp.float32) * jnp.broadcast_to(times, (length, LANES))
                        parts.append((whole - scaled[rows, cols].astype(jnp.float32)).astype(jnp.bfloat16))
                    both = pl.ds(pl.multiple_of(pair * 2 * LANES, 2 * LANES), 2 * LANES)
                    rest[...] += lax.dot_general(
                        jnp.concatenate(parts, axis=1),
                        r_buf[slot, :, both],
                        NT_DIMS,
                        preferred_element_type=jnp.float32,
                    )

                return carry

            lax.fori_loop(0, chunks // 2, one, 0)
            first, second = antidiagonals(rest[...])
            out_ref[0, s, 0:1, :] += first
            out_ref[0, s, 1:2, :] += second


def predict(flags, times, r_shots, s_shots, first_s):
    count_r, count_s = flags.shape[0], len(s_shots)
    length, stations = s_shots[0].shape
    grid_spec = pltpu.PrefetchScalarGridSpec(
        num_scalar_prefetch=1,
        grid=(count_r,),
        in_specs=[
            pl.BlockSpec((1,) + times.shape[1:], lambda i, f: (i, 0, 0, 0)),
            pl.BlockSpec(memory_space=pl.ANY),
        ]
        + [pl.BlockSpec((length, stations), lambda i, f: (0, 0), pipeline_mode=pl.Buffered(1))] * count_s,
        out_specs=pl.BlockSpec((1, count_s, 2, LANES), lambda i, f: (i, 0, 0, 0)),
        scratch_shapes=[
            pltpu.VMEM((count_s * length, stations), jnp.bfloat16),
            pltpu.VMEM((count_s * length, length), jnp.float32),
            pltpu.VMEM((length, length), jnp.float32),
            pltpu.VMEM((2, length, stations), jnp.bfloat16),
            pltpu.SemaphoreType.DMA((2, 4)),
        ],
    )
    return pl.pallas_call(
        functools.partial(pair_kernel, first_s, count_s),
        grid_spec=grid_spec,
        out_shape=jax.ShapeDtypeStruct((count_r, count_s, 2, LANES), jnp.float32),
        compiler_params=pltpu.CompilerParams(vmem_limit_bytes=20 << 20),
        cost_estimate=pl.CostEstimate(flops=2 * 10**9, bytes_accessed=2**20, transcendentals=0),
        name="pairs",
    )(flags, times, r_shots, *s_shots)


def body(signals, aperture, counts):
    length_win, group, stations = signals.shape
    shots = aperture.shape[1]
    slots = aperture.shape[2]
    z, y, c, x = (lax.axis_index(name) for name in AXES)

    live = jnp.arange(slots, dtype=jnp.int32) < counts[:, :, None]
    lists = jnp.where(live, aperture, -1).reshape(group, 16, 2, 4, slots)
    lists = lax.dynamic_index_in_dim(lists, x, 3, keepdims=False)
    mine = lax.dynamic_index_in_dim(lists, c, 2, keepdims=False)
    theirs = from_offset(lax.dynamic_index_in_dim(lists, 1 - c, 2, keepdims=False), dc=1)

    native = lax.optimization_barrier(jnp.transpose(signals, (1, 0, 2)))
    windows = [lax.dynamic_index_in_dim(native, x, 0, keepdims=False)]
    for dx in (1, 2, 3):
        windows.append(from_offset(lax.dynamic_index_in_dim(native, (x - dx) % 4, 0, keepdims=False), dx=dx))
    windows = jnp.stack(windows + windows)
    own = lax.dynamic_slice_in_dim(windows, (4 - x) % 4, 4, 0).reshape(4 * length_win, stations)
    r_shots = lax.all_gather(native, ("c", "x"), axis=0).reshape(2, 4, group, length_win, stations)
    own, mine, theirs = lax.optimization_barrier((own, mine, theirs))

    held = {(0, 0): own}
    blocks = []

    def travel(number):
        for offset, (dz, dy), forwarded in ROUNDS[number]:
            held[offset] = from_offset(held[forwarded], dz=dz, dy=dy)

    def meet(number, others):
        names = [hop[0] for hop in ROUNDS[number]]
        values = lax.optimization_barrier([held[name] for name in names] + list(others))
        held.update(zip(names, values))
        return values[len(names) :]

    def made_of(first_s, count_s):
        s_shots = [held[offset] for offset in S_OFFSETS[first_s : first_s + count_s]]
        return predict(flags, times, r_shots, s_shots, first_s)

    travel(0)
    lists = jnp.stack([mine, theirs]).reshape(2 * group * 16, slots)
    list_rows, made_rows = row_tables()
    device = ((z * 4 + y) * 2 + c) * 4 + x
    rows = lax.dynamic_index_in_dim(jnp.asarray(list_rows), device, 0, keepdims=False)
    lists = lists.at[rows].get(mode="promise_in_bounds").reshape(2 * group, 16, slots)
    times = station_counts(lists)
    whole = times.astype(jnp.int32).reshape(2 * group, 16, 8, 2 * LANES)
    odd = jnp.max((whole & (whole - 1) != 0).astype(jnp.int32), axis=3)
    flags = jnp.sum(odd << jnp.arange(8, dtype=jnp.int32), axis=2)
    flags, times = meet(0, (flags, times))

    travel(1)
    blocks += meet(1, [made_of(0, 5)])
    travel(2)
    blocks += meet(2, [made_of(5, 4)])
    travel(3)
    blocks += meet(3, [made_of(9, 4)])
    blocks.append(made_of(13, 3))
    made = jnp.concatenate(blocks, axis=1).reshape(2 * group * 16, 4 * length_win)

    rows = lax.dynamic_index_in_dim(jnp.asarray(made_rows), device, 0, keepdims=False)
    made = made.at[rows].get(mode="promise_in_bounds").reshape(2, group, 16, 4, length_win)
    made = jnp.transpose(made, (0, 3, 4, 1, 2)).reshape(8, length_win, group, 16)
    made = lax.all_to_all(made, ("c", "x"), 0, 0, tiled=True)
    made = made.reshape(2, 4, length_win, group, 16)
    return jnp.transpose(made, (2, 4, 0, 1, 3)).reshape(length_win, shots, group)


def solution(mesh):
    fine = Mesh(np.asarray(mesh.devices).reshape(SIZES), AXES)
    shot = ("z", "y", "c")
    in_specs = (P("x", shot, None), P(shot, None, None), P(shot, None))
    return jax.shard_map(body, mesh=fine, in_specs=in_specs, out_specs=P("x", None, shot), check_vma=False)
```

```python
import functools
import itertools

import jax
import jax.numpy as jnp
import numpy as np
from jax import lax
from jax.experimental import pallas as pl
from jax.experimental.pallas import tpu as pltpu
from jax.sharding import Mesh
from jax.sharding import PartitionSpec as P

AXES = ("z", "y", "c", "x")
SIZES = (4, 4, 2, 4)
LANES = 128
NT_DIMS = (((1,), (1,)), ((), ()))

ROUNDS = (
    (
        (((0, 1), (0, 1), (0, 0)), ((0, 3), (0, 3), (0, 0))),
        (((1, 0), (1, 0), (0, 0)), ((3, 0), (3, 0), (0, 0))),
    ),
    (
        (((1, 3), (1, 0), (0, 3)), ((3, 1), (3, 0), (0, 1))),
        (((1, 1), (0, 1), (1, 0)), ((3, 3), (0, 3), (3, 0))),
    ),
    (
        (((3, 2), (0, 1), (3, 1)), ((1, 2), (0, 3), (1, 3))),
        (((2, 1), (1, 0), (1, 1)), ((2, 3), (3, 0), (3, 3))),
    ),
    (
        (((0, 2), (1, 0), (3, 2)),),
        (((2, 2), (0, 1), (2, 1)), ((2, 0), (0, 3), (2, 1))),
    ),
)
S_OFFSETS = ((0, 0),) + tuple(hop[0] for parts in ROUNDS for part in parts for hop in part)


def from_offset(value, dz=0, dy=0, dc=0, dx=0):
    pairs = []
    for place in itertools.product(*(range(n) for n in SIZES)):
        source = tuple((p + d) % n for p, d, n in zip(place, (dz, dy, dc, dx), SIZES))
        pairs.append((int(np.ravel_multi_index(source, SIZES)), int(np.ravel_multi_index(place, SIZES))))
    return lax.ppermute(value, AXES, pairs)


def row_tables():
    list_rows, made_rows = [], []
    for z, y, c, x in itertools.product(*(range(n) for n in SIZES)):
        s_slot = [(z + dz) % 4 * 4 + (y + dy) % 4 for dz, dy in S_OFFSETS]
        cores = (0, 1) if c == 0 else (1, 0)
        list_rows.append([(core * 4 + r) * 16 + s for core in cores for r in range(4) for s in s_slot])
        made_rows.append([r * 16 + s_slot.index(s) for r in range(8) for s in range(16)])
    return np.asarray(list_rows, np.int32), np.asarray(made_rows, np.int32)


def count_kernel(list_ref, out_ref):
    stations = list_ref[0]
    high = stations >> 7
    low = stations & (LANES - 1)
    chunk = lax.broadcasted_iota(jnp.int32, (16, LANES), 0)
    lane = lax.broadcasted_iota(jnp.int32, (LANES, LANES), 0)
    for s in range(stations.shape[0]):
        is_high = (high[s : s + 1, :] == chunk).astype(jnp.float32).astype(jnp.bfloat16)
        is_low = (low[s : s + 1, :] == lane).astype(jnp.float32).astype(jnp.bfloat16)
        out_ref[0, s] = lax.dot_general(is_high, is_low, NT_DIMS, preferred_element_type=jnp.float32)


def station_counts(lists):
    count_r, count_s, _ = lists.shape
    return pl.pallas_call(
        count_kernel,
        grid=(count_r,),
        in_specs=[pl.BlockSpec((1, count_s, LANES), lambda i: (i, 0, 0))],
        out_specs=pl.BlockSpec((1, count_s, 16, LANES), lambda i: (i, 0, 0, 0)),
        out_shape=jax.ShapeDtypeStruct((count_r, count_s, 16, LANES), jnp.float32),
        cost_estimate=pl.CostEstimate(flops=10**9, bytes_accessed=2**20, transcendentals=0),
        name="station_counts",
    )(lists)


def antidiagonals(outer):
    tau = lax.broadcasted_iota(jnp.int32, (LANES, LANES), 0)
    lane = lax.broadcasted_iota(jnp.int32, (LANES, LANES), 1)
    keep = lane >= tau
    near = pltpu.roll(outer[:LANES, :LANES], 0, 1, stride=1, stride_axis=0)
    far = outer[:LANES, LANES:] + outer[LANES:, :LANES]
    far = pltpu.roll(far, 0, 1, stride=1, stride_axis=0)
    first = jnp.sum(jnp.where(keep, near, 0.0), axis=0, keepdims=True)
    second = jnp.sum(jnp.where(keep, far, near), axis=0, keepdims=True)
    return first, second


def pair_kernel(first_s, count_s, flag_ref, times_ref, r_ref, *refs):
    s_refs = refs[:count_s]
    out_ref, scaled, outer, rest, r_buf, sems = refs[count_s:]
    length, stations = s_refs[0].shape
    chunks = stations // LANES
    r = pl.program_id(0)
    slot = lax.rem(r, 2)

    def fetch(number, to):
        return pltpu.make_async_copy(r_ref.at[number], r_buf.at[to], sems.at[to])

    @pl.when(r == 0)
    def _():
        fetch(r, 0).start()

    @pl.when(r + 1 < pl.num_programs(0))
    def _():
        fetch(r + 1, 1 - slot).start()

    fetch(r, slot).wait()

    for s in range(count_s):
        for c in range(chunks):
            cols = slice(c * LANES, (c + 1) * LANES)
            times = jnp.broadcast_to(times_ref[0, first_s + s, c : c + 1, :], (16, LANES)).astype(jnp.bfloat16)
            times = jnp.concatenate([times] * (length // 16), axis=0)
            scaled[s * length : (s + 1) * length, cols] = s_refs[s][:, cols] * times
    outer[...] = lax.dot_general(scaled[...], r_buf[slot], NT_DIMS, preferred_element_type=jnp.float32)
    for s in range(count_s):
        first, second = antidiagonals(outer[s * length : (s + 1) * length, :])
        out_ref[0, s, 0:1, :] = first
        out_ref[0, s, 1:2, :] = second

    for s in range(count_s):
        rows = slice(s * length, (s + 1) * length)
        flag = flag_ref[r, first_s + s]

        @pl.when(flag != 0)
        def _():
            rest[...] = jnp.zeros_like(rest)

            def one(pair, carry):
                @pl.when((flag >> pair) & 1 != 0)
                def _():
                    parts = []
                    for half in range(2):
                        cols = pl.ds(pl.multiple_of((pair * 2 + half) * LANES, LANES), LANES)
                        times = times_ref[0, first_s + s, pl.ds(pair * 2 + half, 1), :]
                        whole = s_refs[s][:, cols].astype(jnp.float32) * jnp.broadcast_to(times, (length, LANES))
                        parts.append((whole - scaled[rows, cols].astype(jnp.float32)).astype(jnp.bfloat16))
                    both = pl.ds(pl.multiple_of(pair * 2 * LANES, 2 * LANES), 2 * LANES)
                    rest[...] += lax.dot_general(
                        jnp.concatenate(parts, axis=1),
                        r_buf[slot, :, both],
                        NT_DIMS,
                        preferred_element_type=jnp.float32,
                    )

                return carry

            lax.fori_loop(0, chunks // 2, one, 0)
            first, second = antidiagonals(rest[...])
            out_ref[0, s, 0:1, :] += first
            out_ref[0, s, 1:2, :] += second


def predict(flags, times, r_shots, s_shots, first_s):
    count_r, count_s = flags.shape[0], len(s_shots)
    length, stations = s_shots[0].shape
    grid_spec = pltpu.PrefetchScalarGridSpec(
        num_scalar_prefetch=1,
        grid=(count_r,),
        in_specs=[
            pl.BlockSpec((1,) + times.shape[1:], lambda i, f: (i, 0, 0, 0)),
            pl.BlockSpec(memory_space=pltpu.HBM),
        ]
        + [pl.BlockSpec((length, stations), lambda i, f: (0, 0), pipeline_mode=pl.Buffered(1))] * count_s,
        out_specs=pl.BlockSpec((1, count_s, 2, LANES), lambda i, f: (i, 0, 0, 0)),
        scratch_shapes=[
            pltpu.VMEM((count_s * length, stations), jnp.bfloat16),
            pltpu.VMEM((count_s * length, length), jnp.float32),
            pltpu.VMEM((length, length), jnp.float32),
            pltpu.VMEM((2, length, stations), jnp.bfloat16),
            pltpu.SemaphoreType.DMA((2,)),
        ],
    )
    return pl.pallas_call(
        functools.partial(pair_kernel, first_s, count_s),
        grid_spec=grid_spec,
        out_shape=jax.ShapeDtypeStruct((count_r, count_s, 2, LANES), jnp.float32),
        compiler_params=pltpu.CompilerParams(vmem_limit_bytes=46 << 20),
        cost_estimate=pl.CostEstimate(flops=2 * 10**9, bytes_accessed=2**20, transcendentals=0),
        name="pairs",
    )(flags, times, r_shots, *s_shots)


def body(signals, aperture, counts):
    length_win, group, stations = signals.shape
    shots = aperture.shape[1]
    slots = aperture.shape[2]
    z, y, c, x = (lax.axis_index(name) for name in AXES)

    live = jnp.arange(slots, dtype=jnp.int32) < counts[:, :, None]
    lists = jnp.where(live, aperture, -1).reshape(group, 16, 2, 4, slots)
    lists = lax.dynamic_index_in_dim(lists, x, 3, keepdims=False)
    mine = lax.dynamic_index_in_dim(lists, c, 2, keepdims=False)
    theirs = from_offset(lax.dynamic_index_in_dim(lists, 1 - c, 2, keepdims=False), dc=1)

    native = lax.optimization_barrier(jnp.transpose(signals, (1, 0, 2)))
    windows = [lax.dynamic_index_in_dim(native, x, 0, keepdims=False)]
    for dx in (1, 2, 3):
        windows.append(from_offset(lax.dynamic_index_in_dim(native, (x - dx) % 4, 0, keepdims=False), dx=dx))
    windows = jnp.stack(windows + windows)
    own = lax.dynamic_slice_in_dim(windows, (4 - x) % 4, 4, 0).reshape(4 * length_win, stations)
    own, mine, theirs = lax.optimization_barrier((own, mine, theirs))
    r_shots = lax.all_gather(own, ("c", "x"), axis=0)

    held = {(0, 0): own}
    blocks = []

    def travel(number, part):
        for offset, (dz, dy), forwarded in ROUNDS[number][part]:
            held[offset] = from_offset(held[forwarded], dz=dz, dy=dy)

    def meet(number, part, *others):
        names = [hop[0] for hop in ROUNDS[number][part]]
        values = lax.optimization_barrier([held[name] for name in names] + list(others))
        held.update(zip(names, values))
        return values[len(names) :]

    def made_of(first_s, count_s):
        s_shots = [held[offset] for offset in S_OFFSETS[first_s : first_s + count_s]]
        return predict(flags, times, r_shots, s_shots, first_s)

    travel(0, 0)
    travel(0, 1)
    lists = jnp.stack([mine, theirs]).reshape(2 * group * 16, slots)
    list_rows, made_rows = row_tables()
    device = ((z * 4 + y) * 2 + c) * 4 + x
    rows = lax.dynamic_index_in_dim(jnp.asarray(list_rows), device, 0, keepdims=False)
    lists = lists.at[rows].get(mode="promise_in_bounds").reshape(2 * group, 16, slots)
    times = station_counts(lists)
    whole = times.astype(jnp.int32).reshape(2 * group, 16, 8, 2 * LANES)
    odd = jnp.max((whole & (whole - 1) != 0).astype(jnp.int32), axis=3)
    flags = jnp.sum(odd << jnp.arange(8, dtype=jnp.int32), axis=2)
    flags, times = meet(0, 0, flags, times)
    made = None
    first_s = 0
    for number in range(1, 4):
        travel(number, 0)
        if made is None:
            meet(number - 1, 1)
        else:
            made = meet(number - 1, 1, made)[0]
            blocks.append(made)
        travel(number, 1)
        count_s = 5 if number == 1 else 4
        made = made_of(first_s, count_s)
        first_s += count_s
        made = meet(number, 0, made)[0]
    blocks.append(meet(3, 1, made)[0])
    blocks.append(made_of(first_s, 3))
    made = jnp.concatenate(blocks, axis=1).reshape(2 * group * 16, 4 * length_win)

    rows = lax.dynamic_index_in_dim(jnp.asarray(made_rows), device, 0, keepdims=False)
    made = made.at[rows].get(mode="promise_in_bounds").reshape(2, group, 16, 4, length_win)
    made = jnp.transpose(made, (0, 3, 4, 1, 2)).reshape(8, length_win, group, 16)
    made = lax.all_to_all(made, ("c", "x"), 0, 0, tiled=True)
    made = made.reshape(2, 4, length_win, group, 16)
    return jnp.transpose(made, (2, 4, 0, 1, 3)).reshape(length_win, shots, group)


def solution(mesh):
    fine = Mesh(np.asarray(mesh.devices).reshape(SIZES), AXES)
    shot = ("z", "y", "c")
    in_specs = (P("x", shot, None), P(shot, None, None), P(shot, None))
    return jax.shard_map(body, mesh=fine, in_specs=in_specs, out_specs=P("x", None, shot), check_vma=False)
```

```python
import functools
import itertools

import jax
import jax.numpy as jnp
import numpy as np
from jax import lax
from jax.experimental import pallas as pl
from jax.experimental.pallas import tpu as pltpu
from jax.sharding import Mesh
from jax.sharding import PartitionSpec as P

AXES = ("z", "y", "c", "x")
SIZES = (4, 4, 2, 4)
LANES = 128
NT_DIMS = (((1,), (1,)), ((), ()))

ROUNDS = (
    (((0, 1), (0, 1), (0, 0)), ((0, 3), (0, 3), (0, 0)), ((1, 0), (1, 0), (0, 0)), ((3, 0), (3, 0), (0, 0))),
    (((1, 1), (0, 1), (1, 0)), ((3, 3), (0, 3), (3, 0)), ((1, 3), (1, 0), (0, 3)), ((3, 1), (3, 0), (0, 1))),
    (((0, 2), (0, 1), (0, 1)), ((3, 2), (0, 3), (3, 3)), ((2, 0), (1, 0), (1, 0)), ((2, 1), (3, 0), (3, 1))),
    (((2, 2), (0, 1), (2, 1)), ((1, 2), (0, 3), (1, 3)), ((2, 3), (3, 0), (3, 3))),
)
S_OFFSETS = ((0, 0),) + tuple(hop[0] for hops in ROUNDS for hop in hops)


def from_offset(value, dz=0, dy=0, dc=0, dx=0):
    pairs = []
    for place in itertools.product(*(range(n) for n in SIZES)):
        source = tuple((p + d) % n for p, d, n in zip(place, (dz, dy, dc, dx), SIZES))
        pairs.append((int(np.ravel_multi_index(source, SIZES)), int(np.ravel_multi_index(place, SIZES))))
    return lax.ppermute(value, AXES, pairs)


def row_tables():
    list_rows, made_rows = [], []
    for z, y, c, x in itertools.product(*(range(n) for n in SIZES)):
        s_slot = [(z + dz) % 4 * 4 + (y + dy) % 4 for dz, dy in S_OFFSETS]
        cores = (0, 1) if c == 0 else (1, 0)
        list_rows.append([(core * 4 + r) * 16 + s for core in cores for r in range(4) for s in s_slot])
        made_rows.append([r * 16 + s_slot.index(s) for r in range(8) for s in range(16)])
    return np.asarray(list_rows, np.int32), np.asarray(made_rows, np.int32)


def count_kernel(list_ref, out_ref):
    stations = list_ref[0]
    high = stations >> 7
    low = stations & (LANES - 1)
    chunk = lax.broadcasted_iota(jnp.int32, (16, LANES), 0)
    lane = lax.broadcasted_iota(jnp.int32, (LANES, LANES), 0)
    for s in range(stations.shape[0]):
        is_high = (high[s : s + 1, :] == chunk).astype(jnp.float32).astype(jnp.bfloat16)
        is_low = (low[s : s + 1, :] == lane).astype(jnp.float32).astype(jnp.bfloat16)
        out_ref[0, s] = lax.dot_general(is_high, is_low, NT_DIMS, preferred_element_type=jnp.float32)


def station_counts(lists):
    count_r, count_s, _ = lists.shape
    return pl.pallas_call(
        count_kernel,
        grid=(count_r,),
        in_specs=[pl.BlockSpec((1, count_s, LANES), lambda i: (i, 0, 0))],
        out_specs=pl.BlockSpec((1, count_s, 16, LANES), lambda i: (i, 0, 0, 0)),
        out_shape=jax.ShapeDtypeStruct((count_r, count_s, 16, LANES), jnp.float32),
        cost_estimate=pl.CostEstimate(flops=10**9, bytes_accessed=2**20, transcendentals=0),
        name="station_counts",
    )(lists)


def antidiagonals(outer):
    tau = lax.broadcasted_iota(jnp.int32, (LANES, LANES), 0)
    lane = lax.broadcasted_iota(jnp.int32, (LANES, LANES), 1)
    keep = lane >= tau
    near = pltpu.roll(outer[:LANES, :LANES], 0, 1, stride=1, stride_axis=0)
    far = outer[:LANES, LANES:] + outer[LANES:, :LANES]
    far = pltpu.roll(far, 0, 1, stride=1, stride_axis=0)
    first = jnp.sum(jnp.where(keep, near, 0.0), axis=0, keepdims=True)
    second = jnp.sum(jnp.where(keep, far, near), axis=0, keepdims=True)
    return first, second


def pair_kernel(first_s, count_s, flag_ref, times_ref, r_ref, *refs):
    s_refs = refs[:count_s]
    out_ref, scaled, outer, rest, r_buf, sems = refs[count_s:]
    length, stations = s_refs[0].shape
    _, windows, group, window_len, _ = r_ref.shape
    chunks = stations // LANES
    r = pl.program_id(0)
    slot = lax.rem(r, 2)

    def fetches(number, to):
        for w in range(windows):
            yield pltpu.make_async_copy(
                r_ref.at[number // group, w, lax.rem(number, group)],
                r_buf.at[to, pl.ds(w * window_len, window_len)],
                sems.at[to, w],
            )

    @pl.when(r == 0)
    def _():
        for fetch in fetches(r, 0):
            fetch.start()

    @pl.when(r + 1 < pl.num_programs(0))
    def _():
        for fetch in fetches(r + 1, 1 - slot):
            fetch.start()

    for fetch in fetches(r, slot):
        fetch.wait()

    for s in range(count_s):
        for c in range(chunks):
            cols = slice(c * LANES, (c + 1) * LANES)
            times = jnp.broadcast_to(times_ref[0, first_s + s, c : c + 1, :], (16, LANES)).astype(jnp.bfloat16)
            times = jnp.concatenate([times] * (length // 16), axis=0)
            scaled[s * length : (s + 1) * length, cols] = s_refs[s][:, cols] * times
    outer[...] = lax.dot_general(scaled[...], r_buf[slot], NT_DIMS, preferred_element_type=jnp.float32)
    for s in range(count_s):
        first, second = antidiagonals(outer[s * length : (s + 1) * length, :])
        out_ref[0, s, 0:1, :] = first
        out_ref[0, s, 1:2, :] = second

    for s in range(count_s):
        rows = slice(s * length, (s + 1) * length)
        flag = flag_ref[r, first_s + s]

        @pl.when(flag != 0)
        def _():
            rest[...] = jnp.zeros_like(rest)

            def one(pair, carry):
                @pl.when((flag >> pair) & 1 != 0)
                def _():
                    parts = []
                    for half in range(2):
                        cols = pl.ds(pl.multiple_of((pair * 2 + half) * LANES, LANES), LANES)
                        times = times_ref[0, first_s + s, pl.ds(pair * 2 + half, 1), :]
                        whole = s_refs[s][:, cols].astype(jnp.float32) * jnp.broadcast_to(times, (length, LANES))
                        parts.append((whole - scaled[rows, cols].astype(jnp.float32)).astype(jnp.bfloat16))
                    both = pl.ds(pl.multiple_of(pair * 2 * LANES, 2 * LANES), 2 * LANES)
                    rest[...] += lax.dot_general(
                        jnp.concatenate(parts, axis=1),
                        r_buf[slot, :, both],
                        NT_DIMS,
                        preferred_element_type=jnp.float32,
                    )

                return carry

            lax.fori_loop(0, chunks // 2, one, 0)
            first, second = antidiagonals(rest[...])
            out_ref[0, s, 0:1, :] += first
            out_ref[0, s, 1:2, :] += second


def predict(flags, times, r_shots, s_shots, first_s):
    count_r, count_s = flags.shape[0], len(s_shots)
    length, stations = s_shots[0].shape
    grid_spec = pltpu.PrefetchScalarGridSpec(
        num_scalar_prefetch=1,
        grid=(count_r,),
        in_specs=[
            pl.BlockSpec((1,) + times.shape[1:], lambda i, f: (i, 0, 0, 0)),
            pl.BlockSpec(memory_space=pl.ANY),
        ]
        + [pl.BlockSpec((length, stations), lambda i, f: (0, 0), pipeline_mode=pl.Buffered(1))] * count_s,
        out_specs=pl.BlockSpec((1, count_s, 2, LANES), lambda i, f: (i, 0, 0, 0)),
        scratch_shapes=[
            pltpu.VMEM((count_s * length, stations), jnp.bfloat16),
            pltpu.VMEM((count_s * length, length), jnp.float32),
            pltpu.VMEM((length, length), jnp.float32),
            pltpu.VMEM((2, length, stations), jnp.bfloat16),
            pltpu.SemaphoreType.DMA((2, 4)),
        ],
    )
    return pl.pallas_call(
        functools.partial(pair_kernel, first_s, count_s),
        grid_spec=grid_spec,
        out_shape=jax.ShapeDtypeStruct((count_r, count_s, 2, LANES), jnp.float32),
        compiler_params=pltpu.CompilerParams(vmem_limit_bytes=46 << 20),
        cost_estimate=pl.CostEstimate(flops=2 * 10**9, bytes_accessed=2**20, transcendentals=0),
        name="pairs",
    )(flags, times, r_shots, *s_shots)


def body(signals, aperture, counts):
    length_win, group, stations = signals.shape
    shots = aperture.shape[1]
    slots = aperture.shape[2]
    z, y, c, x = (lax.axis_index(name) for name in AXES)

    live = jnp.arange(slots, dtype=jnp.int32) < counts[:, :, None]
    lists = jnp.where(live, aperture, -1).reshape(group, 16, 2, 4, slots)
    lists = lax.dynamic_index_in_dim(lists, x, 3, keepdims=False)
    mine = lax.dynamic_index_in_dim(lists, c, 2, keepdims=False)
    theirs = from_offset(lax.dynamic_index_in_dim(lists, 1 - c, 2, keepdims=False), dc=1)

    native = lax.optimization_barrier(jnp.transpose(signals, (1, 0, 2)))
    own = lax.all_to_all(native, "x", 0, 0, tiled=True).reshape(4 * length_win, stations)
    r_shots = lax.all_gather(native, ("c", "x"), axis=0).reshape(2, 4, group, length_win, stations)

    held = {(0, 0): own}
    blocks = []

    def travel(number):
        for offset, (dz, dy), forwarded in ROUNDS[number]:
            held[offset] = from_offset(held[forwarded], dz=dz, dy=dy)

    def meet(number, others):
        names = [hop[0] for hop in ROUNDS[number]]
        values = lax.optimization_barrier([held[name] for name in names] + list(others))
        held.update(zip(names, values))
        return values[len(names) :]

    def made_of(first_s, count_s):
        s_shots = [held[offset] for offset in S_OFFSETS[first_s : first_s + count_s]]
        return predict(flags, times, r_shots, s_shots, first_s)

    travel(0)
    lists = jnp.stack([mine, theirs]).reshape(2 * group * 16, slots)
    list_rows, made_rows = row_tables()
    device = ((z * 4 + y) * 2 + c) * 4 + x
    rows = lax.dynamic_index_in_dim(jnp.asarray(list_rows), device, 0, keepdims=False)
    lists = lists.at[rows].get(mode="promise_in_bounds").reshape(2 * group, 16, slots)
    times = station_counts(lists)
    whole = times.astype(jnp.int32).reshape(2 * group, 16, 8, 2 * LANES)
    odd = jnp.max((whole & (whole - 1) != 0).astype(jnp.int32), axis=3)
    flags = jnp.sum(odd << jnp.arange(8, dtype=jnp.int32), axis=2)
    flags, times = meet(0, (flags, times))

    travel(1)
    blocks += meet(1, [made_of(0, 4)])
    travel(2)
    blocks += meet(2, [made_of(4, 5)])
    travel(3)
    blocks += meet(3, [made_of(9, 4)])
    blocks.append(made_of(13, 3))
    made = jnp.concatenate(blocks, axis=1).reshape(2 * group * 16, 4 * length_win)

    rows = lax.dynamic_index_in_dim(jnp.asarray(made_rows), device, 0, keepdims=False)
    made = made.at[rows].get(mode="promise_in_bounds").reshape(2, group, 16, 4, length_win)
    made = jnp.transpose(made, (0, 3, 4, 1, 2)).reshape(8, length_win, group, 16)
    made = lax.all_to_all(made, ("c", "x"), 0, 0, tiled=True)
    made = made.reshape(2, 4, length_win, group, 16)
    return jnp.transpose(made, (2, 4, 0, 1, 3)).reshape(length_win, shots, group)


def solution(mesh):
    fine = Mesh(np.asarray(mesh.devices).reshape(SIZES), AXES)
    shot = ("z", "y", "c")
    in_specs = (P("x", shot, None), P(shot, None, None), P(shot, None))
    return jax.shard_map(body, mesh=fine, in_specs=in_specs, out_specs=P("x", None, shot), check_vma=False)
```

```python
import functools
import itertools

import jax
import jax.numpy as jnp
import numpy as np
from jax import lax
from jax.experimental import pallas as pl
from jax.experimental.pallas import tpu as pltpu
from jax.sharding import Mesh
from jax.sharding import PartitionSpec as P

AXES = ("z", "y", "c", "x")
SIZES = (4, 4, 2, 4)
LANES = 128
GRANT = 46
NT_DIMS = (((1,), (1,)), ((), ()))

ROUNDS = (
    (((0, 1), (0, 1), (0, 0)), ((0, 3), (0, 3), (0, 0)), ((1, 0), (1, 0), (0, 0)), ((3, 0), (3, 0), (0, 0))),
    (((1, 1), (0, 1), (1, 0)), ((3, 3), (0, 3), (3, 0)), ((1, 3), (1, 0), (0, 3)), ((3, 1), (3, 0), (0, 1))),
    (((0, 2), (0, 1), (0, 1)), ((3, 2), (0, 3), (3, 3)), ((2, 0), (1, 0), (1, 0)), ((2, 1), (3, 0), (3, 1))),
    (((2, 2), (0, 1), (2, 1)), ((1, 2), (0, 3), (1, 3)), ((2, 3), (3, 0), (3, 3))),
)
S_OFFSETS = ((0, 0),) + tuple(hop[0] for hops in ROUNDS for hop in hops)


def from_offset(value, dz=0, dy=0, dc=0, dx=0):
    pairs = []
    for place in itertools.product(*(range(n) for n in SIZES)):
        source = tuple((p + d) % n for p, d, n in zip(place, (dz, dy, dc, dx), SIZES))
        pairs.append((int(np.ravel_multi_index(source, SIZES)), int(np.ravel_multi_index(place, SIZES))))
    return lax.ppermute(value, AXES, pairs)


def row_tables():
    list_rows, made_rows = [], []
    for z, y, c, x in itertools.product(*(range(n) for n in SIZES)):
        s_slot = [(z + dz) % 4 * 4 + (y + dy) % 4 for dz, dy in S_OFFSETS]
        cores = (0, 1) if c == 0 else (1, 0)
        list_rows.append([(core * 4 + r) * 16 + s for core in cores for r in range(4) for s in s_slot])
        made_rows.append([r * 16 + s_slot.index(s) for r in range(8) for s in range(16)])
    return np.asarray(list_rows, np.int32), np.asarray(made_rows, np.int32)


def count_kernel(list_ref, out_ref):
    stations = list_ref[0]
    high = stations >> 7
    low = stations & (LANES - 1)
    chunk = lax.broadcasted_iota(jnp.int32, (16, LANES), 0)
    lane = lax.broadcasted_iota(jnp.int32, (LANES, LANES), 0)
    for s in range(stations.shape[0]):
        is_high = (high[s : s + 1, :] == chunk).astype(jnp.float32).astype(jnp.bfloat16)
        is_low = (low[s : s + 1, :] == lane).astype(jnp.float32).astype(jnp.bfloat16)
        out_ref[0, s] = lax.dot_general(is_high, is_low, NT_DIMS, preferred_element_type=jnp.float32)


def station_counts(lists):
    count_r, count_s, _ = lists.shape
    return pl.pallas_call(
        count_kernel,
        grid=(count_r,),
        in_specs=[pl.BlockSpec((1, count_s, LANES), lambda i: (i, 0, 0))],
        out_specs=pl.BlockSpec((1, count_s, 16, LANES), lambda i: (i, 0, 0, 0)),
        out_shape=jax.ShapeDtypeStruct((count_r, count_s, 16, LANES), jnp.float32),
        cost_estimate=pl.CostEstimate(flops=10**9, bytes_accessed=2**20, transcendentals=0),
        name="station_counts",
    )(lists)


def antidiagonals(outer):
    tau = lax.broadcasted_iota(jnp.int32, (LANES, LANES), 0)
    lane = lax.broadcasted_iota(jnp.int32, (LANES, LANES), 1)
    keep = lane >= tau
    near = pltpu.roll(outer[:LANES, :LANES], 0, 1, stride=1, stride_axis=0)
    far = outer[:LANES, LANES:] + outer[LANES:, :LANES]
    far = pltpu.roll(far, 0, 1, stride=1, stride_axis=0)
    first = jnp.sum(jnp.where(keep, near, 0.0), axis=0, keepdims=True)
    second = jnp.sum(jnp.where(keep, far, near), axis=0, keepdims=True)
    return first, second


def pair_kernel(first_s, count_s, flag_ref, times_ref, r_ref, *refs):
    s_refs = refs[:count_s]
    out_ref, scaled, outer, rest, r_buf, sems = refs[count_s:]
    length, stations = s_refs[0].shape
    _, windows, group, window_len, _ = r_ref.shape
    chunks = stations // LANES
    count_r = flag_ref.shape[0]

    def fetches(number, to):
        for w in range(windows):
            yield pltpu.make_async_copy(
                r_ref.at[number // group, w, lax.rem(number, group)],
                r_buf.at[to, pl.ds(w * window_len, window_len)],
                sems.at[to, w],
            )

    for fetch in fetches(0, 0):
        fetch.start()

    def products(r, carry):
        slot = lax.rem(r, 2)

        @pl.when(r + 1 < count_r)
        def _():
            for fetch in fetches(r + 1, 1 - slot):
                fetch.start()

        for fetch in fetches(r, slot):
            fetch.wait()

        for s in range(count_s):
            for c in range(chunks):
                cols = slice(c * LANES, (c + 1) * LANES)
                times = jnp.broadcast_to(times_ref[r, first_s + s, c : c + 1, :], (16, LANES)).astype(jnp.bfloat16)
                times = jnp.concatenate([times] * (length // 16), axis=0)
                scaled[s * length : (s + 1) * length, cols] = s_refs[s][:, cols] * times
        outer[...] = lax.dot_general(scaled[...], r_buf[slot], NT_DIMS, preferred_element_type=jnp.float32)
        for s in range(count_s):
            first, second = antidiagonals(outer[s * length : (s + 1) * length, :])
            out_ref[r, s, 0:1, :] = first
            out_ref[r, s, 1:2, :] = second

        odd = flag_ref[r, first_s]
        for s in range(1, count_s):
            odd = odd | flag_ref[r, first_s + s]

        @pl.when(odd != 0)
        def _():
            for s in range(count_s):
                rows = slice(s * length, (s + 1) * length)
                flag = flag_ref[r, first_s + s]

                @pl.when(flag != 0)
                def _():
                    rest[...] = jnp.zeros_like(rest)

                    def one(pair, carry):
                        @pl.when((flag >> pair) & 1 != 0)
                        def _():
                            parts = []
                            for half in range(2):
                                cols = pl.ds(pl.multiple_of((pair * 2 + half) * LANES, LANES), LANES)
                                times = times_ref[r, first_s + s, pl.ds(pair * 2 + half, 1), :]
                                whole = s_refs[s][:, cols].astype(jnp.float32) * jnp.broadcast_to(times, (length, LANES))
                                parts.append((whole - scaled[rows, cols].astype(jnp.float32)).astype(jnp.bfloat16))
                            both = pl.ds(pl.multiple_of(pair * 2 * LANES, 2 * LANES), 2 * LANES)
                            rest[...] += lax.dot_general(
                                jnp.concatenate(parts, axis=1),
                                r_buf[slot, :, both],
                                NT_DIMS,
                                preferred_element_type=jnp.float32,
                            )

                        return carry

                    lax.fori_loop(0, chunks // 2, one, 0)
                    first, second = antidiagonals(rest[...])
                    out_ref[r, s, 0:1, :] += first
                    out_ref[r, s, 1:2, :] += second

        return carry

    lax.fori_loop(0, count_r, products, 0)


def predict(flags, times, r_shots, s_shots, first_s):
    count_r, count_s = flags.shape[0], len(s_shots)
    length, stations = s_shots[0].shape
    on_chip = pl.BlockSpec(memory_space=pltpu.VMEM)
    return pl.pallas_call(
        functools.partial(pair_kernel, first_s, count_s),
        in_specs=[pl.BlockSpec(memory_space=pltpu.SMEM), on_chip, pl.BlockSpec(memory_space=pltpu.HBM)]
        + [on_chip] * count_s,
        out_specs=on_chip,
        scratch_shapes=[
            pltpu.VMEM((count_s * length, stations), jnp.bfloat16),
            pltpu.VMEM((count_s * length, length), jnp.float32),
            pltpu.VMEM((length, length), jnp.float32),
            pltpu.VMEM((2, length, stations), jnp.bfloat16),
            pltpu.SemaphoreType.DMA((2, 4)),
        ],
        out_shape=jax.ShapeDtypeStruct((count_r, count_s, 2, LANES), jnp.float32),
        compiler_params=pltpu.CompilerParams(vmem_limit_bytes=GRANT << 20),
        cost_estimate=pl.CostEstimate(flops=2 * 10**9, bytes_accessed=2**20, transcendentals=0),
        name="pairs",
    )(flags, times, r_shots, *s_shots)


def body(signals, aperture, counts):
    length_win, group, stations = signals.shape
    shots = aperture.shape[1]
    slots = aperture.shape[2]
    z, y, c, x = (lax.axis_index(name) for name in AXES)

    live = jnp.arange(slots, dtype=jnp.int32) < counts[:, :, None]
    lists = jnp.where(live, aperture, -1).reshape(group, 16, 2, 4, slots)
    lists = lax.dynamic_index_in_dim(lists, x, 3, keepdims=False)
    mine = lax.dynamic_index_in_dim(lists, c, 2, keepdims=False)
    theirs = from_offset(lax.dynamic_index_in_dim(lists, 1 - c, 2, keepdims=False), dc=1)

    native = lax.optimization_barrier(jnp.transpose(signals, (1, 0, 2)))
    own = lax.all_to_all(native, "x", 0, 0, tiled=True).reshape(4 * length_win, stations)
    r_shots = lax.all_gather(native, ("c", "x"), axis=0).reshape(2, 4, group, length_win, stations)

    held = {(0, 0): own}
    blocks = []

    def travel(number):
        for offset, (dz, dy), forwarded in ROUNDS[number]:
            held[offset] = from_offset(held[forwarded], dz=dz, dy=dy)

    def meet(number, others):
        names = [hop[0] for hop in ROUNDS[number]]
        values = lax.optimization_barrier([held[name] for name in names] + list(others))
        held.update(zip(names, values))
        return values[len(names) :]

    def made_of(first_s, count_s):
        s_shots = [held[offset] for offset in S_OFFSETS[first_s : first_s + count_s]]
        return predict(flags, times, r_shots, s_shots, first_s)

    travel(0)
    lists = jnp.stack([mine, theirs]).reshape(2 * group * 16, slots)
    list_rows, made_rows = row_tables()
    device = ((z * 4 + y) * 2 + c) * 4 + x
    rows = lax.dynamic_index_in_dim(jnp.asarray(list_rows), device, 0, keepdims=False)
    lists = lists.at[rows].get(mode="promise_in_bounds").reshape(2 * group, 16, slots)
    times = station_counts(lists)
    whole = times.astype(jnp.int32).reshape(2 * group, 16, 8, 2 * LANES)
    odd = jnp.max((whole & (whole - 1) != 0).astype(jnp.int32), axis=3)
    flags = jnp.sum(odd << jnp.arange(8, dtype=jnp.int32), axis=2)
    (flags,) = meet(0, (flags,))

    travel(1)
    blocks += meet(1, [made_of(0, 4)])
    travel(2)
    blocks += meet(2, [made_of(4, 5)])
    travel(3)
    blocks += meet(3, [made_of(9, 4)])
    blocks.append(made_of(13, 3))
    made = jnp.concatenate(blocks, axis=1).reshape(2 * group * 16, 4 * length_win)

    rows = lax.dynamic_index_in_dim(jnp.asarray(made_rows), device, 0, keepdims=False)
    made = made.at[rows].get(mode="promise_in_bounds").reshape(2, group, 16, 4, length_win)
    made = jnp.transpose(made, (0, 3, 4, 1, 2)).reshape(8, length_win, group, 16)
    made = lax.all_to_all(made, ("c", "x"), 0, 0, tiled=True)
    made = made.reshape(2, 4, length_win, group, 16)
    return jnp.transpose(made, (2, 4, 0, 1, 3)).reshape(length_win, shots, group)


def solution(mesh):
    fine = Mesh(np.asarray(mesh.devices).reshape(SIZES), AXES)
    shot = ("z", "y", "c")
    in_specs = (P("x", shot, None), P(shot, None, None), P(shot, None))
    return jax.shard_map(body, mesh=fine, in_specs=in_specs, out_specs=P("x", None, shot), check_vma=False)
```

```python
import functools
import itertools

import jax
import jax.numpy as jnp
import numpy as np
from jax import lax
from jax.experimental import pallas as pl
from jax.experimental.pallas import tpu as pltpu
from jax.sharding import Mesh
from jax.sharding import PartitionSpec as P

AXES = ("z", "y", "c", "x")
SIZES = (4, 4, 2, 4)
LANES = 128
GRANT = 46
NT_DIMS = (((1,), (1,)), ((), ()))

ROUNDS = (
    (((0, 1), (0, 1), (0, 0)), ((0, 3), (0, 3), (0, 0)), ((1, 0), (1, 0), (0, 0)), ((3, 0), (3, 0), (0, 0))),
    (((1, 1), (0, 1), (1, 0)), ((3, 3), (0, 3), (3, 0)), ((1, 3), (1, 0), (0, 3)), ((3, 1), (3, 0), (0, 1))),
    (((0, 2), (0, 1), (0, 1)), ((3, 2), (0, 3), (3, 3)), ((2, 0), (1, 0), (1, 0)), ((2, 1), (3, 0), (3, 1))),
    (((2, 2), (0, 1), (2, 1)), ((1, 2), (0, 3), (1, 3)), ((2, 3), (3, 0), (3, 3))),
)
S_OFFSETS = ((0, 0),) + tuple(hop[0] for hops in ROUNDS for hop in hops)


def from_offset(value, dz=0, dy=0, dc=0, dx=0):
    pairs = []
    for place in itertools.product(*(range(n) for n in SIZES)):
        source = tuple((p + d) % n for p, d, n in zip(place, (dz, dy, dc, dx), SIZES))
        pairs.append((int(np.ravel_multi_index(source, SIZES)), int(np.ravel_multi_index(place, SIZES))))
    return lax.ppermute(value, AXES, pairs)


def row_tables():
    list_rows, made_rows = [], []
    for z, y, c, x in itertools.product(*(range(n) for n in SIZES)):
        s_slot = [(z + dz) % 4 * 4 + (y + dy) % 4 for dz, dy in S_OFFSETS]
        cores = (0, 1) if c == 0 else (1, 0)
        list_rows.append([(core * 4 + r) * 16 + s for core in cores for r in range(4) for s in s_slot])
        made_rows.append([r * 16 + s_slot.index(s) for r in range(8) for s in range(16)])
    return np.asarray(list_rows, np.int32), np.asarray(made_rows, np.int32)


def count_kernel(list_ref, out_ref):
    count_r, count_s, _ = list_ref.shape
    chunk = lax.broadcasted_iota(jnp.int32, (16, LANES), 0)
    lane = lax.broadcasted_iota(jnp.int32, (LANES, LANES), 0)

    def counts(r, carry):
        stations = list_ref[r]
        high = stations >> 7
        low = stations & (LANES - 1)
        for s in range(count_s):
            is_high = (high[s : s + 1, :] == chunk).astype(jnp.float32).astype(jnp.bfloat16)
            is_low = (low[s : s + 1, :] == lane).astype(jnp.float32).astype(jnp.bfloat16)
            out_ref[r, s] = lax.dot_general(is_high, is_low, NT_DIMS, preferred_element_type=jnp.float32)
        return carry

    lax.fori_loop(0, count_r, counts, 0)


def station_counts(lists):
    count_r, count_s, _ = lists.shape
    on_chip = pl.BlockSpec(memory_space=pltpu.VMEM)
    return pl.pallas_call(
        count_kernel,
        in_specs=[on_chip],
        out_specs=on_chip,
        out_shape=jax.ShapeDtypeStruct((count_r, count_s, 16, LANES), jnp.float32),
        cost_estimate=pl.CostEstimate(flops=10**9, bytes_accessed=2**20, transcendentals=0),
        name="station_counts",
    )(lists)


def antidiagonals(outer):
    tau = lax.broadcasted_iota(jnp.int32, (LANES, LANES), 0)
    lane = lax.broadcasted_iota(jnp.int32, (LANES, LANES), 1)
    keep = lane >= tau
    near = pltpu.roll(outer[:LANES, :LANES], 0, 1, stride=1, stride_axis=0)
    far = outer[:LANES, LANES:] + outer[LANES:, :LANES]
    far = pltpu.roll(far, 0, 1, stride=1, stride_axis=0)
    first = jnp.sum(jnp.where(keep, near, 0.0), axis=0, keepdims=True)
    second = jnp.sum(jnp.where(keep, far, near), axis=0, keepdims=True)
    return first, second


def pair_kernel(first_s, count_s, flag_ref, times_ref, r_ref, *refs):
    s_refs = refs[:count_s]
    out_ref, scaled, outer, times_buf, r_buf, sems = refs[count_s:]
    length, stations = s_refs[0].shape
    _, windows, group, window_len, _ = r_ref.shape
    chunks = stations // LANES
    count_r = flag_ref.shape[0]

    def fetches(number, to):
        for w in range(windows):
            yield pltpu.make_async_copy(
                r_ref.at[number // group, w, lax.rem(number, group)],
                r_buf.at[to, pl.ds(w * window_len, window_len)],
                sems.at[to, w],
            )
        yield pltpu.make_async_copy(
            times_ref.at[number, pl.ds(first_s, count_s)], times_buf.at[to], sems.at[to, windows]
        )

    for fetch in fetches(0, 0):
        fetch.start()

    def products(r, carry):
        slot = lax.rem(r, 2)

        @pl.when(r + 1 < count_r)
        def _():
            for fetch in fetches(r + 1, 1 - slot):
                fetch.start()

        for fetch in fetches(r, slot):
            fetch.wait()

        for s in range(count_s):
            for c in range(chunks):
                cols = slice(c * LANES, (c + 1) * LANES)
                times = jnp.broadcast_to(times_buf[slot, s, c : c + 1, :], (16, LANES)).astype(jnp.bfloat16)
                times = jnp.concatenate([times] * (length // 16), axis=0)
                scaled[s * length : (s + 1) * length, cols] = s_refs[s][:, cols] * times
        outer[...] = lax.dot_general(scaled[...], r_buf[slot], NT_DIMS, preferred_element_type=jnp.float32)
        for s in range(count_s):
            first, second = antidiagonals(outer[s * length : (s + 1) * length, :])
            out_ref[r, s, 0:1, :] = first
            out_ref[r, s, 1:2, :] = second

        odd = flag_ref[r, first_s]
        for s in range(1, count_s):
            odd = odd | flag_ref[r, first_s + s]

        @pl.when(odd != 0)
        def _():
            for s in range(count_s):
                rows = slice(s * length, (s + 1) * length)
                flag = flag_ref[r, first_s + s]

                @pl.when(flag != 0)
                def _():
                    def one(pair, carry):
                        @pl.when((flag >> pair) & 1 != 0)
                        def _():
                            parts = []
                            for half in range(2):
                                cols = pl.ds(pl.multiple_of((pair * 2 + half) * LANES, LANES), LANES)
                                times = times_buf[slot, s, pl.ds(pair * 2 + half, 1), :]
                                whole = s_refs[s][:, cols].astype(jnp.float32) * jnp.broadcast_to(times, (length, LANES))
                                parts.append((whole - scaled[rows, cols].astype(jnp.float32)).astype(jnp.bfloat16))
                            both = pl.ds(pl.multiple_of(pair * 2 * LANES, 2 * LANES), 2 * LANES)
                            rest = lax.dot_general(
                                jnp.concatenate(parts, axis=1),
                                r_buf[slot, :, both],
                                NT_DIMS,
                                preferred_element_type=jnp.float32,
                            )
                            first, second = antidiagonals(rest)
                            out_ref[r, s, 0:1, :] += first
                            out_ref[r, s, 1:2, :] += second

                        return carry

                    lax.fori_loop(0, chunks // 2, one, 0)

        return carry

    lax.fori_loop(0, count_r, products, 0)


def predict(flags, times, r_shots, s_shots, first_s):
    count_r, count_s = flags.shape[0], len(s_shots)
    length, stations = s_shots[0].shape
    on_chip = pl.BlockSpec(memory_space=pltpu.VMEM)
    return pl.pallas_call(
        functools.partial(pair_kernel, first_s, count_s),
        in_specs=[pl.BlockSpec(memory_space=pltpu.SMEM)]
        + [pl.BlockSpec(memory_space=pltpu.HBM)] * 2
        + [on_chip] * count_s,
        out_specs=on_chip,
        scratch_shapes=[
            pltpu.VMEM((count_s * length, stations), jnp.bfloat16),
            pltpu.VMEM((count_s * length, length), jnp.float32),
            pltpu.VMEM((2, count_s) + times.shape[2:], jnp.float32),
            pltpu.VMEM((2, length, stations), jnp.bfloat16),
            pltpu.SemaphoreType.DMA((2, 5)),
        ],
        out_shape=jax.ShapeDtypeStruct((count_r, count_s, 2, LANES), jnp.float32),
        compiler_params=pltpu.CompilerParams(vmem_limit_bytes=GRANT << 20),
        cost_estimate=pl.CostEstimate(flops=2 * 10**9, bytes_accessed=2**20, transcendentals=0),
        name="pairs",
    )(flags, times, r_shots, *s_shots)


def body(signals, aperture, counts):
    length_win, group, stations = signals.shape
    shots = aperture.shape[1]
    slots = aperture.shape[2]
    z, y, c, x = (lax.axis_index(name) for name in AXES)

    live = jnp.arange(slots, dtype=jnp.int32) < counts[:, :, None]
    lists = jnp.where(live, aperture, -1).reshape(group, 16, 2, 4, slots)
    lists = lax.dynamic_index_in_dim(lists, x, 3, keepdims=False)
    mine = lax.dynamic_index_in_dim(lists, c, 2, keepdims=False)
    theirs = from_offset(lax.dynamic_index_in_dim(lists, 1 - c, 2, keepdims=False), dc=1)

    native = lax.optimization_barrier(jnp.transpose(signals, (1, 0, 2)))
    own = lax.all_to_all(native, "x", 0, 0, tiled=True).reshape(4 * length_win, stations)
    r_shots = lax.all_gather(native, ("c", "x"), axis=0).reshape(2, 4, group, length_win, stations)

    held = {(0, 0): own}
    blocks = []

    def travel(number):
        for offset, (dz, dy), forwarded in ROUNDS[number]:
            held[offset] = from_offset(held[forwarded], dz=dz, dy=dy)

    def meet(number, others):
        names = [hop[0] for hop in ROUNDS[number]]
        values = lax.optimization_barrier([held[name] for name in names] + list(others))
        held.update(zip(names, values))
        return values[len(names) :]

    def made_of(first_s, count_s):
        s_shots = [held[offset] for offset in S_OFFSETS[first_s : first_s + count_s]]
        return predict(flags, times, r_shots, s_shots, first_s)

    travel(0)
    lists = jnp.stack([mine, theirs]).reshape(2 * group * 16, slots)
    list_rows, made_rows = row_tables()
    device = ((z * 4 + y) * 2 + c) * 4 + x
    rows = lax.dynamic_index_in_dim(jnp.asarray(list_rows), device, 0, keepdims=False)
    lists = lists.at[rows].get(mode="promise_in_bounds").reshape(2 * group, 16, slots)
    times = station_counts(lists)
    whole = times.astype(jnp.int32).reshape(2 * group, 16, 8, 2 * LANES)
    odd = jnp.max((whole & (whole - 1) != 0).astype(jnp.int32), axis=3)
    flags = jnp.sum(odd << jnp.arange(8, dtype=jnp.int32), axis=2)
    (flags,) = meet(0, (flags,))

    travel(1)
    blocks += meet(1, [made_of(0, 4)])
    travel(2)
    blocks += meet(2, [made_of(4, 5)])
    travel(3)
    blocks += meet(3, [made_of(9, 4)])
    blocks.append(made_of(13, 3))
    made = jnp.concatenate(blocks, axis=1).reshape(2 * group * 16, 4 * length_win)

    rows = lax.dynamic_index_in_dim(jnp.asarray(made_rows), device, 0, keepdims=False)
    made = made.at[rows].get(mode="promise_in_bounds").reshape(2, group, 16, 4, length_win)
    made = jnp.transpose(made, (0, 3, 4, 1, 2)).reshape(8, -1, LANES)
    made = lax.all_to_all(made, ("c", "x"), 0, 0, tiled=True)
    made = made.reshape(2, 4, length_win, group, 16)
    return jnp.transpose(made, (2, 4, 0, 1, 3)).reshape(length_win, shots, group)


def solution(mesh):
    fine = Mesh(np.asarray(mesh.devices).reshape(SIZES), AXES)
    shot = ("z", "y", "c")
    in_specs = (P("x", shot, None), P(shot, None, None), P(shot, None))
    return jax.shard_map(body, mesh=fine, in_specs=in_specs, out_specs=P("x", None, shot), check_vma=False)
```

```python
import functools
import itertools

import jax
import jax.numpy as jnp
import numpy as np
from jax import lax
from jax.experimental import pallas as pl
from jax.experimental.pallas import tpu as pltpu
from jax.sharding import Mesh
from jax.sharding import PartitionSpec as P

AXES = ("z", "y", "c", "x")
SIZES = (4, 4, 2, 4)
LANES = 128
GRANT = 46
NT_DIMS = (((1,), (1,)), ((), ()))

ROUNDS = (
    (((0, 1), (0, 1), (0, 0)), ((0, 3), (0, 3), (0, 0)), ((1, 0), (1, 0), (0, 0)), ((3, 0), (3, 0), (0, 0))),
    (((1, 1), (0, 1), (1, 0)), ((3, 3), (0, 3), (3, 0)), ((1, 3), (1, 0), (0, 3)), ((3, 1), (3, 0), (0, 1))),
    (((0, 2), (0, 1), (0, 1)), ((3, 2), (0, 3), (3, 3)), ((2, 0), (1, 0), (1, 0)), ((2, 1), (3, 0), (3, 1))),
    (((2, 2), (0, 1), (2, 1)), ((1, 2), (0, 3), (1, 3)), ((2, 3), (3, 0), (3, 3))),
)
S_OFFSETS = ((0, 0),) + tuple(hop[0] for hops in ROUNDS for hop in hops)


def from_offset(value, dz=0, dy=0, dc=0, dx=0):
    pairs = []
    for place in itertools.product(*(range(n) for n in SIZES)):
        source = tuple((p + d) % n for p, d, n in zip(place, (dz, dy, dc, dx), SIZES))
        pairs.append((int(np.ravel_multi_index(source, SIZES)), int(np.ravel_multi_index(place, SIZES))))
    return lax.ppermute(value, AXES, pairs)


def row_tables():
    list_rows, made_rows = [], []
    for z, y, c, x in itertools.product(*(range(n) for n in SIZES)):
        s_slot = [(z + dz) % 4 * 4 + (y + dy) % 4 for dz, dy in S_OFFSETS]
        cores = (0, 1) if c == 0 else (1, 0)
        list_rows.append([(core * 4 + r) * 16 + s for core in cores for r in range(4) for s in s_slot])
        made_rows.append([r * 16 + s_slot.index(s) for r in range(8) for s in range(16)])
    return np.asarray(list_rows, np.int32), np.asarray(made_rows, np.int32)


def count_kernel(list_ref, out_ref):
    count_r, count_s, _ = list_ref.shape
    chunk = lax.broadcasted_iota(jnp.int32, (16, LANES), 0)
    lane = lax.broadcasted_iota(jnp.int32, (LANES, LANES), 0)

    def counts(r, carry):
        stations = list_ref[r]
        high = stations >> 7
        low = stations & (LANES - 1)
        for s in range(count_s):
            is_high = (high[s : s + 1, :] == chunk).astype(jnp.float32).astype(jnp.bfloat16)
            is_low = (low[s : s + 1, :] == lane).astype(jnp.float32).astype(jnp.bfloat16)
            out_ref[r, s] = lax.dot_general(is_high, is_low, NT_DIMS, preferred_element_type=jnp.float32)
        return carry

    lax.fori_loop(0, count_r, counts, 0)


def station_counts(lists):
    count_r, count_s, _ = lists.shape
    on_chip = pl.BlockSpec(memory_space=pltpu.VMEM)
    return pl.pallas_call(
        count_kernel,
        in_specs=[on_chip],
        out_specs=on_chip,
        out_shape=jax.ShapeDtypeStruct((count_r, count_s, 16, LANES), jnp.float32),
        cost_estimate=pl.CostEstimate(flops=10**9, bytes_accessed=2**20, transcendentals=0),
        name="station_counts",
    )(lists)


def antidiagonals(outer):
    tau = lax.broadcasted_iota(jnp.int32, (LANES, LANES), 0)
    lane = lax.broadcasted_iota(jnp.int32, (LANES, LANES), 1)
    keep = lane >= tau
    near = pltpu.roll(outer[:LANES, :LANES], 0, 1, stride=1, stride_axis=0)
    far = outer[:LANES, LANES:] + outer[LANES:, :LANES]
    far = pltpu.roll(far, 0, 1, stride=1, stride_axis=0)
    first = jnp.sum(jnp.where(keep, near, 0.0), axis=0, keepdims=True)
    second = jnp.sum(jnp.where(keep, far, near), axis=0, keepdims=True)
    return first, second


def pair_kernel(first_s, count_s, flag_ref, times_ref, r_ref, *refs):
    s_refs = refs[:count_s]
    out_ref, scaled, outer, times_buf, r_buf, sems = refs[count_s:]
    length, stations = s_refs[0].shape
    _, windows, group, window_len, _ = r_ref.shape
    chunks = stations // LANES
    count_r = flag_ref.shape[0]

    def fetches(number, to):
        for w in range(windows):
            yield pltpu.make_async_copy(
                r_ref.at[number // group, w, lax.rem(number, group)],
                r_buf.at[to, pl.ds(w * window_len, window_len)],
                sems.at[to, w],
            )
        yield pltpu.make_async_copy(
            times_ref.at[number, pl.ds(first_s, count_s)], times_buf.at[to], sems.at[to, windows]
        )

    for fetch in fetches(0, 0):
        fetch.start()

    def products(r, carry):
        slot = lax.rem(r, 2)

        @pl.when(r + 1 < count_r)
        def _():
            for fetch in fetches(r + 1, 1 - slot):
                fetch.start()

        for fetch in fetches(r, slot):
            fetch.wait()

        for s in range(count_s):
            for c in range(chunks):
                cols = slice(c * LANES, (c + 1) * LANES)
                times = jnp.broadcast_to(times_buf[slot, s, c : c + 1, :], (16, LANES)).astype(jnp.bfloat16)
                times = jnp.concatenate([times] * (length // 16), axis=0)
                scaled[s * length : (s + 1) * length, cols] = s_refs[s][:, cols] * times
        outer[...] = lax.dot_general(scaled[...], r_buf[slot], NT_DIMS, preferred_element_type=jnp.float32)
        for s in range(count_s):
            first, second = antidiagonals(outer[s * length : (s + 1) * length, :])
            out_ref[r, s, 0:1, :] = first
            out_ref[r, s, 1:2, :] = second

        odd = flag_ref[r, first_s]
        for s in range(1, count_s):
            odd = odd | flag_ref[r, first_s + s]

        @pl.when(odd != 0)
        def _():
            for s in range(count_s):
                rows = slice(s * length, (s + 1) * length)
                flag = flag_ref[r, first_s + s]

                @pl.when(flag != 0)
                def _():
                    def one(pair, carry):
                        @pl.when((flag >> pair) & 1 != 0)
                        def _():
                            parts = []
                            for half in range(2):
                                cols = pl.ds(pl.multiple_of((pair * 2 + half) * LANES, LANES), LANES)
                                times = times_buf[slot, s, pl.ds(pair * 2 + half, 1), :]
                                whole = s_refs[s][:, cols].astype(jnp.float32) * jnp.broadcast_to(times, (length, LANES))
                                parts.append((whole - scaled[rows, cols].astype(jnp.float32)).astype(jnp.bfloat16))
                            both = pl.ds(pl.multiple_of(pair * 2 * LANES, 2 * LANES), 2 * LANES)
                            rest = lax.dot_general(
                                jnp.concatenate(parts, axis=1),
                                r_buf[slot, :, both],
                                NT_DIMS,
                                preferred_element_type=jnp.float32,
                            )
                            first, second = antidiagonals(rest)
                            out_ref[r, s, 0:1, :] += first
                            out_ref[r, s, 1:2, :] += second

                        return carry

                    lax.fori_loop(0, chunks // 2, one, 0)

        return carry

    lax.fori_loop(0, count_r, products, 0)


def predict(flags, times, r_shots, s_shots, first_s):
    count_r, count_s = flags.shape[0], len(s_shots)
    length, stations = s_shots[0].shape
    on_chip = pl.BlockSpec(memory_space=pltpu.VMEM)
    return pl.pallas_call(
        functools.partial(pair_kernel, first_s, count_s),
        in_specs=[pl.BlockSpec(memory_space=pltpu.SMEM)]
        + [pl.BlockSpec(memory_space=pltpu.HBM)] * 2
        + [on_chip] * count_s,
        out_specs=on_chip,
        scratch_shapes=[
            pltpu.VMEM((count_s * length, stations), jnp.bfloat16),
            pltpu.VMEM((count_s * length, length), jnp.float32),
            pltpu.VMEM((2, count_s) + times.shape[2:], jnp.float32),
            pltpu.VMEM((2, length, stations), jnp.bfloat16),
            pltpu.SemaphoreType.DMA((2, 5)),
        ],
        out_shape=jax.ShapeDtypeStruct((count_r, count_s, 2, LANES), jnp.float32),
        compiler_params=pltpu.CompilerParams(vmem_limit_bytes=GRANT << 20),
        cost_estimate=pl.CostEstimate(flops=2 * 10**9, bytes_accessed=2**20, transcendentals=0),
        name="pairs",
    )(flags, times, r_shots, *s_shots)


def body(signals, aperture, counts):
    length_win, group, stations = signals.shape
    shots = aperture.shape[1]
    slots = aperture.shape[2]
    z, y, c, x = (lax.axis_index(name) for name in AXES)

    live = jnp.arange(slots, dtype=jnp.int32) < counts[:, :, None]
    lists = jnp.where(live, aperture, -1).reshape(group, 16, 2, 4, slots)
    lists = lax.dynamic_index_in_dim(lists, x, 3, keepdims=False)
    mine = lax.dynamic_index_in_dim(lists, c, 2, keepdims=False)
    theirs = from_offset(lax.dynamic_index_in_dim(lists, 1 - c, 2, keepdims=False), dc=1)

    native = lax.optimization_barrier(jnp.transpose(signals, (1, 0, 2)))
    own = lax.all_to_all(native, "x", 0, 0, tiled=True).reshape(4 * length_win, stations)
    r_shots = lax.all_gather(native, ("c", "x"), axis=0).reshape(2, 4, group, length_win, stations)

    held = {(0, 0): own}
    blocks = []

    def travel(number):
        for offset, (dz, dy), forwarded in ROUNDS[number]:
            held[offset] = from_offset(held[forwarded], dz=dz, dy=dy)

    def meet(number, others):
        names = [hop[0] for hop in ROUNDS[number]]
        values = lax.optimization_barrier([held[name] for name in names] + list(others))
        held.update(zip(names, values))
        return values[len(names) :]

    def made_of(first_s, count_s):
        s_shots = [held[offset] for offset in S_OFFSETS[first_s : first_s + count_s]]
        return predict(flags, times, r_shots, s_shots, first_s)

    travel(0)
    lists = jnp.stack([mine, theirs]).reshape(2 * group * 16, slots)
    list_rows, made_rows = row_tables()
    device = ((z * 4 + y) * 2 + c) * 4 + x
    rows = lax.dynamic_index_in_dim(jnp.asarray(list_rows), device, 0, keepdims=False)
    lists = lists.at[rows].get(mode="promise_in_bounds").reshape(2 * group, 16, slots)
    times = station_counts(lists)
    whole = times.astype(jnp.int32).reshape(2 * group, 16, 8, 2 * LANES)
    odd = jnp.max((whole & (whole - 1) != 0).astype(jnp.int32), axis=3)
    flags = jnp.sum(odd << jnp.arange(8, dtype=jnp.int32), axis=2)
    made_row = lax.dynamic_index_in_dim(jnp.asarray(made_rows), device, 0, keepdims=False)
    flags, made_row = meet(0, (flags, made_row))

    travel(1)
    blocks += meet(1, [made_of(0, 3)])
    travel(2)
    blocks += meet(2, [made_of(3, 6)])
    travel(3)
    blocks += meet(3, [made_of(9, 4)])
    blocks.append(made_of(13, 3))
    made = jnp.concatenate(blocks, axis=1).reshape(2 * group * 16, 4 * length_win)

    made = made.at[made_row].get(mode="promise_in_bounds").reshape(2, group, 16, 4, length_win)
    made = jnp.transpose(made, (0, 3, 4, 1, 2)).reshape(8, -1, LANES)
    made = lax.all_to_all(made, ("c", "x"), 0, 0, tiled=True)
    made = made.reshape(2, 4, length_win, group, 16)
    return jnp.transpose(made, (2, 4, 0, 1, 3)).reshape(length_win, shots, group)


def solution(mesh):
    fine = Mesh(np.asarray(mesh.devices).reshape(SIZES), AXES)
    shot = ("z", "y", "c")
    in_specs = (P("x", shot, None), P(shot, None, None), P(shot, None))
    return jax.shard_map(body, mesh=fine, in_specs=in_specs, out_specs=P("x", None, shot), check_vma=False)
```

```python
import functools
import itertools

import jax
import jax.numpy as jnp
import numpy as np
from jax import lax
from jax.experimental import pallas as pl
from jax.experimental.pallas import tpu as pltpu
from jax.sharding import Mesh
from jax.sharding import PartitionSpec as P

AXES = ("z", "y", "c", "x")
SIZES = (4, 4, 2, 4)
LANES = 128
GRANT = 46
NT_DIMS = (((1,), (1,)), ((), ()))

ROUNDS = (
    (((0, 1), (0, 1), (0, 0)), ((0, 3), (0, 3), (0, 0)), ((1, 0), (1, 0), (0, 0)), ((3, 0), (3, 0), (0, 0))),
    (((1, 1), (0, 1), (1, 0)), ((3, 3), (0, 3), (3, 0)), ((1, 3), (1, 0), (0, 3)), ((3, 1), (3, 0), (0, 1))),
    (((0, 2), (0, 1), (0, 1)), ((3, 2), (0, 3), (3, 3)), ((2, 0), (1, 0), (1, 0)), ((2, 1), (3, 0), (3, 1))),
    (((2, 2), (0, 1), (2, 1)), ((1, 2), (0, 3), (1, 3)), ((2, 3), (3, 0), (3, 3))),
)
S_OFFSETS = ((0, 0),) + tuple(hop[0] for hops in ROUNDS for hop in hops)


def from_offset(value, dz=0, dy=0, dc=0, dx=0):
    pairs = []
    for place in itertools.product(*(range(n) for n in SIZES)):
        source = tuple((p + d) % n for p, d, n in zip(place, (dz, dy, dc, dx), SIZES))
        pairs.append((int(np.ravel_multi_index(source, SIZES)), int(np.ravel_multi_index(place, SIZES))))
    return lax.ppermute(value, AXES, pairs)


def row_tables():
    list_rows, made_rows = [], []
    for z, y, c, x in itertools.product(*(range(n) for n in SIZES)):
        s_slot = [(z + dz) % 4 * 4 + (y + dy) % 4 for dz, dy in S_OFFSETS]
        cores = (0, 1) if c == 0 else (1, 0)
        list_rows.append([(core * 4 + r) * 16 + s for core in cores for r in range(4) for s in s_slot])
        made_rows.append([r * 16 + s_slot.index(s) for r in range(8) for s in range(16)])
    return np.asarray(list_rows, np.int32), np.asarray(made_rows, np.int32)


def count_kernel(list_ref, out_ref):
    count_r, count_s, _ = list_ref.shape
    chunk = lax.broadcasted_iota(jnp.int32, (16, LANES), 0)
    lane = lax.broadcasted_iota(jnp.int32, (LANES, LANES), 0)

    def counts(r, carry):
        stations = list_ref[r]
        high = stations >> 7
        low = stations & (LANES - 1)
        for s in range(count_s):
            is_high = (high[s : s + 1, :] == chunk).astype(jnp.float32).astype(jnp.bfloat16)
            is_low = (low[s : s + 1, :] == lane).astype(jnp.float32).astype(jnp.bfloat16)
            out_ref[r, s] = lax.dot_general(is_high, is_low, NT_DIMS, preferred_element_type=jnp.float32)
        return carry

    lax.fori_loop(0, count_r, counts, 0)


def station_counts(lists):
    count_r, count_s, _ = lists.shape
    on_chip = pl.BlockSpec(memory_space=pltpu.VMEM)
    return pl.pallas_call(
        count_kernel,
        in_specs=[on_chip],
        out_specs=on_chip,
        out_shape=jax.ShapeDtypeStruct((count_r, count_s, 16, LANES), jnp.float32),
        cost_estimate=pl.CostEstimate(flops=10**9, bytes_accessed=2**20, transcendentals=0),
        name="station_counts",
    )(lists)


def antidiagonals(outer):
    tau = lax.broadcasted_iota(jnp.int32, (LANES, LANES), 0)
    lane = lax.broadcasted_iota(jnp.int32, (LANES, LANES), 1)
    keep = lane >= tau
    near = pltpu.roll(outer[:LANES, :LANES], 0, 1, stride=1, stride_axis=0)
    far = outer[:LANES, LANES:] + outer[LANES:, :LANES]
    far = pltpu.roll(far, 0, 1, stride=1, stride_axis=0)
    first = jnp.sum(jnp.where(keep, near, 0.0), axis=0, keepdims=True)
    second = jnp.sum(jnp.where(keep, far, near), axis=0, keepdims=True)
    return first, second


def pair_kernel(first_s, count_s, flag_ref, times_ref, r_ref, *refs):
    s_refs = refs[:count_s]
    out_ref, scaled, outer, times_buf, r_buf, sems = refs[count_s:]
    length, stations = s_refs[0].shape
    _, windows, group, window_len, _ = r_ref.shape
    chunks = stations // LANES
    count_r = flag_ref.shape[0]

    def fetches(number, to):
        for w in range(windows):
            yield pltpu.make_async_copy(
                r_ref.at[number // group, w, lax.rem(number, group)],
                r_buf.at[to, pl.ds(w * window_len, window_len)],
                sems.at[to, w],
            )
        yield pltpu.make_async_copy(
            times_ref.at[number, pl.ds(first_s, count_s)], times_buf.at[to], sems.at[to, windows]
        )

    for fetch in fetches(0, 0):
        fetch.start()

    def products(r, carry):
        slot = lax.rem(r, 2)

        @pl.when(r + 1 < count_r)
        def _():
            for fetch in fetches(r + 1, 1 - slot):
                fetch.start()

        for fetch in fetches(r, slot):
            fetch.wait()

        for s in range(count_s):
            for c in range(chunks):
                cols = slice(c * LANES, (c + 1) * LANES)
                times = jnp.broadcast_to(times_buf[slot, s, c : c + 1, :], (16, LANES)).astype(jnp.bfloat16)
                times = jnp.concatenate([times] * (length // 16), axis=0)
                scaled[s * length : (s + 1) * length, cols] = s_refs[s][:, cols] * times
        outer[...] = lax.dot_general(scaled[...], r_buf[slot], NT_DIMS, preferred_element_type=jnp.float32)
        for s in range(count_s):
            first, second = antidiagonals(outer[s * length : (s + 1) * length, :])
            out_ref[r, s, 0:1, :] = first
            out_ref[r, s, 1:2, :] = second

        odd = flag_ref[r, first_s]
        for s in range(1, count_s):
            odd = odd | flag_ref[r, first_s + s]

        @pl.when(odd != 0)
        def _():
            for s in range(count_s):
                rows = slice(s * length, (s + 1) * length)
                flag = flag_ref[r, first_s + s]

                @pl.when(flag != 0)
                def _():
                    def one(pair, carry):
                        @pl.when((flag >> pair) & 1 != 0)
                        def _():
                            parts = []
                            for half in range(2):
                                cols = pl.ds(pl.multiple_of((pair * 2 + half) * LANES, LANES), LANES)
                                times = times_buf[slot, s, pl.ds(pair * 2 + half, 1), :]
                                whole = s_refs[s][:, cols].astype(jnp.float32) * jnp.broadcast_to(times, (length, LANES))
                                parts.append((whole - scaled[rows, cols].astype(jnp.float32)).astype(jnp.bfloat16))
                            both = pl.ds(pl.multiple_of(pair * 2 * LANES, 2 * LANES), 2 * LANES)
                            rest = lax.dot_general(
                                jnp.concatenate(parts, axis=1),
                                r_buf[slot, :, both],
                                NT_DIMS,
                                preferred_element_type=jnp.float32,
                            )
                            first, second = antidiagonals(rest)
                            out_ref[r, s, 0:1, :] += first
                            out_ref[r, s, 1:2, :] += second

                        return carry

                    lax.fori_loop(0, chunks // 2, one, 0)

        return carry

    lax.fori_loop(0, count_r, products, 0)


def predict(flags, times, r_shots, s_shots, first_s):
    count_r, count_s = flags.shape[0], len(s_shots)
    length, stations = s_shots[0].shape
    on_chip = pl.BlockSpec(memory_space=pltpu.VMEM)
    return pl.pallas_call(
        functools.partial(pair_kernel, first_s, count_s),
        in_specs=[pl.BlockSpec(memory_space=pltpu.SMEM)]
        + [pl.BlockSpec(memory_space=pltpu.HBM)] * 2
        + [on_chip] * count_s,
        out_specs=on_chip,
        scratch_shapes=[
            pltpu.VMEM((count_s * length, stations), jnp.bfloat16),
            pltpu.VMEM((count_s * length, length), jnp.float32),
            pltpu.VMEM((2, count_s) + times.shape[2:], jnp.float32),
            pltpu.VMEM((2, length, stations), jnp.bfloat16),
            pltpu.SemaphoreType.DMA((2, 5)),
        ],
        out_shape=jax.ShapeDtypeStruct((count_r, count_s, 2, LANES), jnp.float32),
        compiler_params=pltpu.CompilerParams(vmem_limit_bytes=GRANT << 20),
        cost_estimate=pl.CostEstimate(flops=2 * 10**9, bytes_accessed=2**20, transcendentals=0),
        name="pairs",
    )(flags, times, r_shots, *s_shots)


def body(signals, aperture, counts):
    length_win, group, stations = signals.shape
    shots = aperture.shape[1]
    slots = aperture.shape[2]
    z, y, c, x = (lax.axis_index(name) for name in AXES)

    live = jnp.arange(slots, dtype=jnp.int32) < counts[:, :, None]
    lists = jnp.where(live, aperture, -1).reshape(group, 16, 2, 4, slots)
    lists = lax.dynamic_index_in_dim(lists, x, 3, keepdims=False)
    mine = lax.dynamic_index_in_dim(lists, c, 2, keepdims=False)
    theirs = from_offset(lax.dynamic_index_in_dim(lists, 1 - c, 2, keepdims=False), dc=1)

    native = lax.optimization_barrier(jnp.transpose(signals, (1, 0, 2)))
    windows = {0: lax.dynamic_index_in_dim(native, x, 0)}
    for dx in (1, 3, 2):
        windows[dx] = from_offset(lax.dynamic_index_in_dim(native, (x - dx) % 4, 0), dx=dx)
    windows[1], later = lax.optimization_barrier((windows[1], native))
    own = jnp.zeros_like(native)
    for dx, window in windows.items():
        own = lax.dynamic_update_slice_in_dim(own, window, (x + dx) % 4, 0)
    own = own.reshape(4 * length_win, stations)
    r_shots = lax.all_gather(later, ("c", "x"), axis=0).reshape(2, 4, group, length_win, stations)

    held = {(0, 0): own}
    blocks = []

    def travel(number):
        for offset, (dz, dy), forwarded in ROUNDS[number]:
            held[offset] = from_offset(held[forwarded], dz=dz, dy=dy)

    def meet(number, others):
        names = [hop[0] for hop in ROUNDS[number]]
        values = lax.optimization_barrier([held[name] for name in names] + list(others))
        held.update(zip(names, values))
        return values[len(names) :]

    def made_of(first_s, count_s):
        s_shots = [held[offset] for offset in S_OFFSETS[first_s : first_s + count_s]]
        return predict(flags, times, r_shots, s_shots, first_s)

    travel(0)
    lists = jnp.stack([mine, theirs]).reshape(2 * group * 16, slots)
    list_rows, made_rows = row_tables()
    device = ((z * 4 + y) * 2 + c) * 4 + x
    rows = lax.dynamic_index_in_dim(jnp.asarray(list_rows), device, 0, keepdims=False)
    lists = lists.at[rows].get(mode="promise_in_bounds").reshape(2 * group, 16, slots)
    times = station_counts(lists)
    whole = times.astype(jnp.int32).reshape(2 * group, 16, 8, 2 * LANES)
    odd = jnp.max((whole & (whole - 1) != 0).astype(jnp.int32), axis=3)
    flags = jnp.sum(odd << jnp.arange(8, dtype=jnp.int32), axis=2)
    made_row = lax.dynamic_index_in_dim(jnp.asarray(made_rows), device, 0, keepdims=False)
    flags, made_row = meet(0, (flags, made_row))

    travel(1)
    blocks += meet(1, [made_of(0, 3)])
    travel(2)
    blocks += meet(2, [made_of(3, 6)])
    travel(3)
    blocks += meet(3, [made_of(9, 4)])
    blocks.append(made_of(13, 3))
    made = jnp.concatenate(blocks, axis=1).reshape(2 * group * 16, 4 * length_win)

    made = made.at[made_row].get(mode="promise_in_bounds").reshape(2, group, 16, 4, length_win)
    made = jnp.transpose(made, (0, 3, 4, 1, 2)).reshape(8, -1, LANES)
    made = lax.all_to_all(made, ("c", "x"), 0, 0, tiled=True)
    made = made.reshape(2, 4, length_win, group, 16)
    return jnp.transpose(made, (2, 4, 0, 1, 3)).reshape(length_win, shots, group)


def solution(mesh):
    fine = Mesh(np.asarray(mesh.devices).reshape(SIZES), AXES)
    shot = ("z", "y", "c")
    in_specs = (P("x", shot, None), P(shot, None, None), P(shot, None))
    return jax.shard_map(body, mesh=fine, in_specs=in_specs, out_specs=P("x", None, shot), check_vma=False)
```

```python
import functools
import itertools

import jax
import jax.numpy as jnp
import numpy as np
from jax import lax
from jax.experimental import pallas as pl
from jax.experimental.pallas import tpu as pltpu
from jax.sharding import Mesh
from jax.sharding import PartitionSpec as P

AXES = ("z", "y", "c", "x")
SIZES = (4, 4, 2, 4)
LANES = 128
GRANT = 46
NT_DIMS = (((1,), (1,)), ((), ()))

ROUNDS = (
    (((0, 1), (0, 1), (0, 0)), ((0, 3), (0, 3), (0, 0)), ((1, 0), (1, 0), (0, 0)), ((3, 0), (3, 0), (0, 0))),
    (((1, 1), (0, 1), (1, 0)), ((3, 3), (0, 3), (3, 0)), ((1, 3), (1, 0), (0, 3)), ((3, 1), (3, 0), (0, 1))),
    (((0, 2), (0, 1), (0, 1)), ((3, 2), (0, 3), (3, 3)), ((2, 0), (1, 0), (1, 0)), ((2, 1), (3, 0), (3, 1))),
    (((2, 2), (0, 1), (2, 1)), ((2, 3), (1, 0), (1, 3)), ((1, 2), (0, 3), (1, 3))),
)
S_OFFSETS = ((0, 0),) + tuple(hop[0] for hops in ROUNDS for hop in hops)


def from_offset(value, dz=0, dy=0, dc=0, dx=0):
    pairs = []
    for place in itertools.product(*(range(n) for n in SIZES)):
        source = tuple((p + d) % n for p, d, n in zip(place, (dz, dy, dc, dx), SIZES))
        pairs.append((int(np.ravel_multi_index(source, SIZES)), int(np.ravel_multi_index(place, SIZES))))
    return lax.ppermute(value, AXES, pairs)


def row_tables():
    list_rows, made_rows = [], []
    for z, y, c, x in itertools.product(*(range(n) for n in SIZES)):
        s_slot = [(z + dz) % 4 * 4 + (y + dy) % 4 for dz, dy in S_OFFSETS]
        cores = (0, 1) if c == 0 else (1, 0)
        list_rows.append([(core * 4 + r) * 16 + s for core in cores for r in range(4) for s in s_slot])
        made_rows.append([r * 16 + s_slot.index(s) for r in range(8) for s in range(16)])
    return np.asarray(list_rows, np.int32), np.asarray(made_rows, np.int32)


def count_kernel(list_ref, out_ref):
    count_r, count_s, _ = list_ref.shape
    chunk = lax.broadcasted_iota(jnp.int32, (16, LANES), 0)
    lane = lax.broadcasted_iota(jnp.int32, (LANES, LANES), 0)

    def counts(r, carry):
        stations = list_ref[r]
        high = stations >> 7
        low = stations & (LANES - 1)
        for s in range(count_s):
            is_high = (high[s : s + 1, :] == chunk).astype(jnp.float32).astype(jnp.bfloat16)
            is_low = (low[s : s + 1, :] == lane).astype(jnp.float32).astype(jnp.bfloat16)
            out_ref[r, s] = lax.dot_general(is_high, is_low, NT_DIMS, preferred_element_type=jnp.float32)
        return carry

    lax.fori_loop(0, count_r, counts, 0)


def station_counts(lists):
    count_r, count_s, _ = lists.shape
    on_chip = pl.BlockSpec(memory_space=pltpu.VMEM)
    return pl.pallas_call(
        count_kernel,
        in_specs=[on_chip],
        out_specs=on_chip,
        out_shape=jax.ShapeDtypeStruct((count_r, count_s, 16, LANES), jnp.float32),
        cost_estimate=pl.CostEstimate(flops=10**9, bytes_accessed=2**20, transcendentals=0),
        name="station_counts",
    )(lists)


def antidiagonals(outer):
    tau = lax.broadcasted_iota(jnp.int32, (LANES, LANES), 0)
    lane = lax.broadcasted_iota(jnp.int32, (LANES, LANES), 1)
    keep = lane >= tau
    near = pltpu.roll(outer[:LANES, :LANES], 0, 1, stride=1, stride_axis=0)
    far = outer[:LANES, LANES:] + outer[LANES:, :LANES]
    far = pltpu.roll(far, 0, 1, stride=1, stride_axis=0)
    first = jnp.sum(jnp.where(keep, near, 0.0), axis=0, keepdims=True)
    second = jnp.sum(jnp.where(keep, far, near), axis=0, keepdims=True)
    return first, second


def pair_kernel(first_s, count_s, flag_ref, times_ref, r_ref, *refs):
    s_refs = refs[:count_s]
    out_ref, scaled, outer, times_buf, r_buf, sems = refs[count_s:]
    length, stations = s_refs[0].shape
    _, windows, group, window_len, _ = r_ref.shape
    chunks = stations // LANES
    count_r = flag_ref.shape[0]

    def fetches(number, to):
        for w in range(windows):
            yield pltpu.make_async_copy(
                r_ref.at[number // group, w, lax.rem(number, group)],
                r_buf.at[to, pl.ds(w * window_len, window_len)],
                sems.at[to, w],
            )
        yield pltpu.make_async_copy(
            times_ref.at[number, pl.ds(first_s, count_s)], times_buf.at[to], sems.at[to, windows]
        )

    for fetch in fetches(0, 0):
        fetch.start()

    def products(r, carry):
        slot = lax.rem(r, 2)

        @pl.when(r + 1 < count_r)
        def _():
            for fetch in fetches(r + 1, 1 - slot):
                fetch.start()

        for fetch in fetches(r, slot):
            fetch.wait()

        for s in range(count_s):
            for c in range(chunks):
                cols = slice(c * LANES, (c + 1) * LANES)
                times = jnp.broadcast_to(times_buf[slot, s, c : c + 1, :], (16, LANES)).astype(jnp.bfloat16)
                times = jnp.concatenate([times] * (length // 16), axis=0)
                scaled[s * length : (s + 1) * length, cols] = s_refs[s][:, cols] * times
        outer[...] = lax.dot_general(scaled[...], r_buf[slot], NT_DIMS, preferred_element_type=jnp.float32)
        for s in range(count_s):
            first, second = antidiagonals(outer[s * length : (s + 1) * length, :])
            out_ref[r, s, 0:1, :] = first
            out_ref[r, s, 1:2, :] = second

        odd = flag_ref[r, first_s]
        for s in range(1, count_s):
            odd = odd | flag_ref[r, first_s + s]

        @pl.when(odd != 0)
        def _():
            for s in range(count_s):
                rows = slice(s * length, (s + 1) * length)
                flag = flag_ref[r, first_s + s]

                @pl.when(flag != 0)
                def _():
                    def one(pair, carry):
                        @pl.when((flag >> pair) & 1 != 0)
                        def _():
                            parts = []
                            for half in range(2):
                                cols = pl.ds(pl.multiple_of((pair * 2 + half) * LANES, LANES), LANES)
                                times = times_buf[slot, s, pl.ds(pair * 2 + half, 1), :]
                                whole = s_refs[s][:, cols].astype(jnp.float32) * jnp.broadcast_to(times, (length, LANES))
                                parts.append((whole - scaled[rows, cols].astype(jnp.float32)).astype(jnp.bfloat16))
                            both = pl.ds(pl.multiple_of(pair * 2 * LANES, 2 * LANES), 2 * LANES)
                            rest = lax.dot_general(
                                jnp.concatenate(parts, axis=1),
                                r_buf[slot, :, both],
                                NT_DIMS,
                                preferred_element_type=jnp.float32,
                            )
                            first, second = antidiagonals(rest)
                            out_ref[r, s, 0:1, :] += first
                            out_ref[r, s, 1:2, :] += second

                        return carry

                    lax.fori_loop(0, chunks // 2, one, 0)

        return carry

    lax.fori_loop(0, count_r, products, 0)


def predict(flags, times, r_shots, s_shots, first_s):
    count_r, count_s = flags.shape[0], len(s_shots)
    length, stations = s_shots[0].shape
    on_chip = pl.BlockSpec(memory_space=pltpu.VMEM)
    return pl.pallas_call(
        functools.partial(pair_kernel, first_s, count_s),
        in_specs=[pl.BlockSpec(memory_space=pltpu.SMEM)]
        + [pl.BlockSpec(memory_space=pltpu.HBM)] * 2
        + [on_chip] * count_s,
        out_specs=on_chip,
        scratch_shapes=[
            pltpu.VMEM((count_s * length, stations), jnp.bfloat16),
            pltpu.VMEM((count_s * length, length), jnp.float32),
            pltpu.VMEM((2, count_s) + times.shape[2:], jnp.float32),
            pltpu.VMEM((2, length, stations), jnp.bfloat16),
            pltpu.SemaphoreType.DMA((2, 5)),
        ],
        out_shape=jax.ShapeDtypeStruct((count_r, count_s, 2, LANES), jnp.float32),
        compiler_params=pltpu.CompilerParams(vmem_limit_bytes=GRANT << 20),
        cost_estimate=pl.CostEstimate(flops=2 * 10**9, bytes_accessed=2**20, transcendentals=0),
        name="pairs",
    )(flags, times, r_shots, *s_shots)


def body(signals, aperture, counts):
    length_win, group, stations = signals.shape
    shots = aperture.shape[1]
    slots = aperture.shape[2]
    z, y, c, x = (lax.axis_index(name) for name in AXES)

    live = jnp.arange(slots, dtype=jnp.int32) < counts[:, :, None]
    lists = jnp.where(live, aperture, -1).reshape(group, 16, 2, 4, slots)
    lists = lax.dynamic_index_in_dim(lists, x, 3, keepdims=False)
    mine = lax.dynamic_index_in_dim(lists, c, 2, keepdims=False)
    theirs = from_offset(lax.dynamic_index_in_dim(lists, 1 - c, 2, keepdims=False), dc=1)

    native = lax.optimization_barrier(jnp.transpose(signals, (1, 0, 2)))
    own = lax.all_to_all(native, "x", 0, 0, tiled=True).reshape(4 * length_win, stations)
    r_shots = lax.all_gather(native, ("c", "x"), axis=0).reshape(2, 4, group, length_win, stations)

    held = {(0, 0): own}
    blocks = []

    def travel(number):
        for offset, (dz, dy), forwarded in ROUNDS[number]:
            held[offset] = from_offset(held[forwarded], dz=dz, dy=dy)

    def meet(number, others):
        names = [hop[0] for hop in ROUNDS[number]]
        values = lax.optimization_barrier([held[name] for name in names] + list(others))
        held.update(zip(names, values))
        return values[len(names) :]

    def made_of(first_s, count_s):
        s_shots = [held[offset] for offset in S_OFFSETS[first_s : first_s + count_s]]
        return predict(flags, times, r_shots, s_shots, first_s)

    travel(0)
    lists = jnp.stack([mine, theirs]).reshape(2 * group * 16, slots)
    list_rows, made_rows = row_tables()
    device = ((z * 4 + y) * 2 + c) * 4 + x
    rows = lax.dynamic_index_in_dim(jnp.asarray(list_rows), device, 0, keepdims=False)
    lists = lists.at[rows].get(mode="promise_in_bounds").reshape(2 * group, 16, slots)
    times = station_counts(lists)
    whole = times.astype(jnp.int32).reshape(2 * group, 16, 8, 2 * LANES)
    odd = jnp.max((whole & (whole - 1) != 0).astype(jnp.int32), axis=3)
    flags = jnp.sum(odd << jnp.arange(8, dtype=jnp.int32), axis=2)
    made_row = lax.dynamic_index_in_dim(jnp.asarray(made_rows), device, 0, keepdims=False)
    flags, made_row = meet(0, (flags, made_row))

    travel(1)
    blocks += meet(1, [made_of(0, 3)])
    travel(2)
    blocks += meet(2, [made_of(3, 6)])
    travel(3)
    blocks += meet(3, [made_of(9, 4)])
    blocks.append(made_of(13, 3))
    made = jnp.concatenate(blocks, axis=1).reshape(2 * group * 16, 4 * length_win)

    made = made.at[made_row].get(mode="promise_in_bounds").reshape(2, group, 16, 4, length_win)
    made = jnp.transpose(made, (0, 3, 4, 1, 2)).reshape(8, -1, LANES)
    made = lax.all_to_all(made, ("c", "x"), 0, 0, tiled=True)
    made = made.reshape(2, 4, length_win, group, 16)
    return jnp.transpose(made, (2, 4, 0, 1, 3)).reshape(length_win, shots, group)


def solution(mesh):
    fine = Mesh(np.asarray(mesh.devices).reshape(SIZES), AXES)
    shot = ("z", "y", "c")
    in_specs = (P("x", shot, None), P(shot, None, None), P(shot, None))
    return jax.shard_map(body, mesh=fine, in_specs=in_specs, out_specs=P("x", None, shot), check_vma=False)
```

```python
import functools
import itertools

import jax
import jax.numpy as jnp
import numpy as np
from jax import lax
from jax.experimental import pallas as pl
from jax.experimental.pallas import tpu as pltpu
from jax.sharding import Mesh
from jax.sharding import PartitionSpec as P

AXES = ("z", "y", "c", "x")
SIZES = (4, 4, 2, 4)
LANES = 128
GRANT = 46
NT_DIMS = (((1,), (1,)), ((), ()))

ROUNDS = (
    (((0, 1), (0, 1), (0, 0)), ((0, 3), (0, 3), (0, 0)), ((1, 0), (1, 0), (0, 0)), ((3, 0), (3, 0), (0, 0))),
    (((1, 1), (0, 1), (1, 0)), ((3, 3), (0, 3), (3, 0)), ((1, 3), (1, 0), (0, 3)), ((3, 1), (3, 0), (0, 1))),
    (((0, 2), (0, 1), (0, 1)), ((3, 2), (0, 3), (3, 3)), ((2, 0), (1, 0), (1, 0)), ((2, 1), (3, 0), (3, 1))),
    (((2, 2), (0, 1), (2, 1)), ((1, 2), (0, 3), (1, 3)), ((2, 3), (3, 0), (3, 3))),
)
S_OFFSETS = ((0, 0),) + tuple(hop[0] for hops in ROUNDS for hop in hops)


def from_offset(value, dz=0, dy=0, dc=0, dx=0):
    pairs = []
    for place in itertools.product(*(range(n) for n in SIZES)):
        source = tuple((p + d) % n for p, d, n in zip(place, (dz, dy, dc, dx), SIZES))
        pairs.append((int(np.ravel_multi_index(source, SIZES)), int(np.ravel_multi_index(place, SIZES))))
    return lax.ppermute(value, AXES, pairs)


def row_tables():
    list_rows, made_rows = [], []
    for z, y, c, x in itertools.product(*(range(n) for n in SIZES)):
        s_slot = [(z + dz) % 4 * 4 + (y + dy) % 4 for dz, dy in S_OFFSETS]
        cores = (0, 1) if c == 0 else (1, 0)
        list_rows.append([(core * 4 + r) * 16 + s for core in cores for r in range(4) for s in s_slot])
        made_rows.append([r * 16 + s_slot.index(s) for r in range(8) for s in range(16)])
    return np.asarray(list_rows, np.int32), np.asarray(made_rows, np.int32)


def count_kernel(list_ref, out_ref):
    count_r, count_s, _ = list_ref.shape
    chunk = lax.broadcasted_iota(jnp.int32, (16, LANES), 0)
    lane = lax.broadcasted_iota(jnp.int32, (LANES, LANES), 0)

    def counts(r, carry):
        stations = list_ref[r]
        high = stations >> 7
        low = stations & (LANES - 1)
        for s in range(count_s):
            is_high = (high[s : s + 1, :] == chunk).astype(jnp.float32).astype(jnp.bfloat16)
            is_low = (low[s : s + 1, :] == lane).astype(jnp.float32).astype(jnp.bfloat16)
            out_ref[r, s] = lax.dot_general(is_high, is_low, NT_DIMS, preferred_element_type=jnp.float32)
        return carry

    lax.fori_loop(0, count_r, counts, 0)


def station_counts(lists):
    count_r, count_s, _ = lists.shape
    on_chip = pl.BlockSpec(memory_space=pltpu.VMEM)
    return pl.pallas_call(
        count_kernel,
        in_specs=[on_chip],
        out_specs=on_chip,
        out_shape=jax.ShapeDtypeStruct((count_r, count_s, 16, LANES), jnp.float32),
        cost_estimate=pl.CostEstimate(flops=10**9, bytes_accessed=2**20, transcendentals=0),
        name="station_counts",
    )(lists)


def antidiagonals(outer):
    tau = lax.broadcasted_iota(jnp.int32, (LANES, LANES), 0)
    lane = lax.broadcasted_iota(jnp.int32, (LANES, LANES), 1)
    keep = lane >= tau
    near = pltpu.roll(outer[:LANES, :LANES], 0, 1, stride=1, stride_axis=0)
    far = outer[:LANES, LANES:] + outer[LANES:, :LANES]
    far = pltpu.roll(far, 0, 1, stride=1, stride_axis=0)
    first = jnp.sum(jnp.where(keep, near, 0.0), axis=0, keepdims=True)
    second = jnp.sum(jnp.where(keep, far, near), axis=0, keepdims=True)
    return first, second


def pair_kernel(first_s, count_s, flag_ref, times_ref, r_ref, *refs):
    s_refs = refs[:count_s]
    out_ref, scaled, outer, times_buf, r_buf, sems = refs[count_s:]
    length, stations = s_refs[0].shape
    _, windows, group, window_len, _ = r_ref.shape
    chunks = stations // LANES
    count_r = flag_ref.shape[0]

    def fetches(number, to):
        for w in range(windows):
            yield pltpu.make_async_copy(
                r_ref.at[number // group, w, lax.rem(number, group)],
                r_buf.at[to, pl.ds(w * window_len, window_len)],
                sems.at[to, w],
            )
        yield pltpu.make_async_copy(
            times_ref.at[number, pl.ds(first_s, count_s)], times_buf.at[to], sems.at[to, windows]
        )

    for fetch in fetches(0, 0):
        fetch.start()

    def products(r, carry):
        slot = lax.rem(r, 2)

        @pl.when(r + 1 < count_r)
        def _():
            for fetch in fetches(r + 1, 1 - slot):
                fetch.start()

        for fetch in fetches(r, slot):
            fetch.wait()

        for s in range(count_s):
            for c in range(chunks):
                cols = slice(c * LANES, (c + 1) * LANES)
                times = jnp.broadcast_to(times_buf[slot, s, c : c + 1, :], (16, LANES)).astype(jnp.bfloat16)
                times = jnp.concatenate([times] * (length // 16), axis=0)
                scaled[s * length : (s + 1) * length, cols] = s_refs[s][:, cols] * times
        outer[...] = lax.dot_general(scaled[...], r_buf[slot], NT_DIMS, preferred_element_type=jnp.float32)
        for s in range(count_s):
            first, second = antidiagonals(outer[s * length : (s + 1) * length, :])
            out_ref[r, s, 0:1, :] = first
            out_ref[r, s, 1:2, :] = second

        odd = flag_ref[r, first_s]
        for s in range(1, count_s):
            odd = odd | flag_ref[r, first_s + s]

        @pl.when(odd != 0)
        def _():
            for s in range(count_s):
                rows = slice(s * length, (s + 1) * length)
                flag = flag_ref[r, first_s + s]

                @pl.when(flag != 0)
                def _():
                    def one(pair, carry):
                        @pl.when((flag >> pair) & 1 != 0)
                        def _():
                            parts = []
                            for half in range(2):
                                cols = pl.ds(pl.multiple_of((pair * 2 + half) * LANES, LANES), LANES)
                                times = times_buf[slot, s, pl.ds(pair * 2 + half, 1), :]
                                whole = s_refs[s][:, cols].astype(jnp.float32) * jnp.broadcast_to(times, (length, LANES))
                                parts.append((whole - scaled[rows, cols].astype(jnp.float32)).astype(jnp.bfloat16))
                            both = pl.ds(pl.multiple_of(pair * 2 * LANES, 2 * LANES), 2 * LANES)
                            rest = lax.dot_general(
                                jnp.concatenate(parts, axis=1),
                                r_buf[slot, :, both],
                                NT_DIMS,
                                preferred_element_type=jnp.float32,
                            )
                            first, second = antidiagonals(rest)
                            out_ref[r, s, 0:1, :] += first
                            out_ref[r, s, 1:2, :] += second

                        return carry

                    lax.fori_loop(0, chunks // 2, one, 0)

        return carry

    lax.fori_loop(0, count_r, products, 0)


def predict(flags, times, r_shots, s_shots, first_s):
    count_r, count_s = flags.shape[0], len(s_shots)
    length, stations = s_shots[0].shape
    on_chip = pl.BlockSpec(memory_space=pltpu.VMEM)
    return pl.pallas_call(
        functools.partial(pair_kernel, first_s, count_s),
        in_specs=[pl.BlockSpec(memory_space=pltpu.SMEM)]
        + [pl.BlockSpec(memory_space=pltpu.HBM)] * 2
        + [on_chip] * count_s,
        out_specs=on_chip,
        scratch_shapes=[
            pltpu.VMEM((count_s * length, stations), jnp.bfloat16),
            pltpu.VMEM((count_s * length, length), jnp.float32),
            pltpu.VMEM((2, count_s) + times.shape[2:], jnp.float32),
            pltpu.VMEM((2, length, stations), jnp.bfloat16),
            pltpu.SemaphoreType.DMA((2, 5)),
        ],
        out_shape=jax.ShapeDtypeStruct((count_r, count_s, 2, LANES), jnp.float32),
        compiler_params=pltpu.CompilerParams(vmem_limit_bytes=GRANT << 20),
        cost_estimate=pl.CostEstimate(flops=2 * 10**9, bytes_accessed=2**20, transcendentals=0),
        name="pairs",
    )(flags, times, r_shots, *s_shots)


def body(signals, aperture, counts):
    length_win, group, stations = signals.shape
    shots = aperture.shape[1]
    slots = aperture.shape[2]
    z, y, c, x = (lax.axis_index(name) for name in AXES)

    live = jnp.arange(slots, dtype=jnp.int32) < counts[:, :, None]
    lists = jnp.where(live, aperture, -1).reshape(group, 16, 2, 4, slots)
    lists = lax.dynamic_index_in_dim(lists, x, 3, keepdims=False)
    mine = lax.dynamic_index_in_dim(lists, c, 2, keepdims=False)
    theirs = from_offset(lax.dynamic_index_in_dim(lists, 1 - c, 2, keepdims=False), dc=1)

    native = lax.optimization_barrier(jnp.transpose(signals, (1, 0, 2)))
    own = lax.all_to_all(native, "x", 0, 0, tiled=True).reshape(4 * length_win, stations)
    r_shots = lax.all_gather(native, ("c", "x"), axis=0).reshape(2, 4, group, length_win, stations)

    held = {(0, 0): own}
    blocks = []

    def travel(number):
        for offset, (dz, dy), forwarded in ROUNDS[number]:
            held[offset] = from_offset(held[forwarded], dz=dz, dy=dy)

    def meet(number, others):
        names = list(held) if number == 1 else [hop[0] for hop in ROUNDS[number]]
        values = lax.optimization_barrier([held[name] for name in names] + list(others))
        held.update(zip(names, values))
        return values[len(names) :]

    def made_of(first_s, count_s):
        s_shots = [held[offset] for offset in S_OFFSETS[first_s : first_s + count_s]]
        return predict(flags, times, r_shots, s_shots, first_s)

    travel(0)
    lists = jnp.stack([mine, theirs]).reshape(2 * group * 16, slots)
    list_rows, made_rows = row_tables()
    device = ((z * 4 + y) * 2 + c) * 4 + x
    rows = lax.dynamic_index_in_dim(jnp.asarray(list_rows), device, 0, keepdims=False)
    lists = lists.at[rows].get(mode="promise_in_bounds").reshape(2 * group, 16, slots)
    times = station_counts(lists)
    whole = times.astype(jnp.int32).reshape(2 * group, 16, 8, 2 * LANES)
    odd = jnp.max((whole & (whole - 1) != 0).astype(jnp.int32), axis=3)
    flags = jnp.sum(odd << jnp.arange(8, dtype=jnp.int32), axis=2)
    made_row = lax.dynamic_index_in_dim(jnp.asarray(made_rows), device, 0, keepdims=False)
    flags, made_row = meet(0, (flags, made_row))

    travel(1)
    blocks += meet(1, [made_of(0, 3)])
    travel(2)
    blocks += meet(2, [made_of(3, 6)])
    travel(3)
    blocks += meet(3, [made_of(9, 4)])
    blocks.append(made_of(13, 3))
    made = jnp.concatenate(blocks, axis=1).reshape(2 * group * 16, 4 * length_win)

    made = made.at[made_row].get(mode="promise_in_bounds").reshape(2, group, 16, 4, length_win)
    made = jnp.transpose(made, (0, 3, 4, 1, 2)).reshape(8, -1, LANES)
    made = lax.all_to_all(made, ("c", "x"), 0, 0, tiled=True)
    made = made.reshape(2, 4, length_win, group, 16)
    return jnp.transpose(made, (2, 4, 0, 1, 3)).reshape(length_win, shots, group)


def solution(mesh):
    fine = Mesh(np.asarray(mesh.devices).reshape(SIZES), AXES)
    shot = ("z", "y", "c")
    in_specs = (P("x", shot, None), P(shot, None, None), P(shot, None))
    return jax.shard_map(body, mesh=fine, in_specs=in_specs, out_specs=P("x", None, shot), check_vma=False)
```

```python
import functools
import itertools

import jax
import jax.numpy as jnp
import numpy as np
from jax import lax
from jax.experimental import pallas as pl
from jax.experimental.pallas import tpu as pltpu
from jax.sharding import Mesh
from jax.sharding import PartitionSpec as P

AXES = ("z", "y", "c", "x")
SIZES = (4, 4, 2, 4)
LANES = 128
GRANT = 46
NT_DIMS = (((1,), (1,)), ((), ()))

ROUNDS = (
    (((0, 1), (0, 1), (0, 0)), ((0, 3), (0, 3), (0, 0)), ((1, 0), (1, 0), (0, 0)), ((3, 0), (3, 0), (0, 0))),
    (((1, 1), (0, 1), (1, 0)), ((3, 3), (0, 3), (3, 0)), ((1, 3), (1, 0), (0, 3)), ((3, 1), (3, 0), (0, 1))),
    (((0, 2), (0, 1), (0, 1)), ((3, 2), (0, 3), (3, 3)), ((2, 0), (1, 0), (1, 0)), ((2, 1), (3, 0), (3, 1))),
    (((2, 2), (0, 1), (2, 1)), ((1, 2), (0, 3), (1, 3)), ((2, 3), (3, 0), (3, 3))),
)
S_OFFSETS = ((0, 0),) + tuple(hop[0] for hops in ROUNDS for hop in hops)


def from_offset(value, dz=0, dy=0, dc=0, dx=0):
    pairs = []
    for place in itertools.product(*(range(n) for n in SIZES)):
        source = tuple((p + d) % n for p, d, n in zip(place, (dz, dy, dc, dx), SIZES))
        pairs.append((int(np.ravel_multi_index(source, SIZES)), int(np.ravel_multi_index(place, SIZES))))
    return lax.ppermute(value, AXES, pairs)


def row_tables():
    list_rows, made_rows = [], []
    for z, y, c, x in itertools.product(*(range(n) for n in SIZES)):
        s_slot = [(z + dz) % 4 * 4 + (y + dy) % 4 for dz, dy in S_OFFSETS]
        cores = (0, 1) if c == 0 else (1, 0)
        list_rows.append([(core * 4 + r) * 16 + s for core in cores for r in range(4) for s in s_slot])
        made_rows.append([r * 16 + s_slot.index(s) for r in range(8) for s in range(16)])
    return np.asarray(list_rows, np.int32), np.asarray(made_rows, np.int32)


def count_kernel(list_ref, out_ref):
    count_r, count_s, _ = list_ref.shape
    chunk = lax.broadcasted_iota(jnp.int32, (16, LANES), 0)
    lane = lax.broadcasted_iota(jnp.int32, (LANES, LANES), 0)

    def counts(r, carry):
        stations = list_ref[r]
        high = stations >> 7
        low = stations & (LANES - 1)
        for s in range(count_s):
            is_high = (high[s : s + 1, :] == chunk).astype(jnp.float32).astype(jnp.bfloat16)
            is_low = (low[s : s + 1, :] == lane).astype(jnp.float32).astype(jnp.bfloat16)
            out_ref[r, s] = lax.dot_general(is_high, is_low, NT_DIMS, preferred_element_type=jnp.float32)
        return carry

    lax.fori_loop(0, count_r, counts, 0)


def station_counts(lists):
    count_r, count_s, _ = lists.shape
    on_chip = pl.BlockSpec(memory_space=pltpu.VMEM)
    return pl.pallas_call(
        count_kernel,
        in_specs=[on_chip],
        out_specs=on_chip,
        out_shape=jax.ShapeDtypeStruct((count_r, count_s, 16, LANES), jnp.float32),
        cost_estimate=pl.CostEstimate(flops=10**9, bytes_accessed=2**20, transcendentals=0),
        name="station_counts",
    )(lists)


def antidiagonals(outer):
    tau = lax.broadcasted_iota(jnp.int32, (LANES, LANES), 0)
    lane = lax.broadcasted_iota(jnp.int32, (LANES, LANES), 1)
    keep = lane >= tau
    near = pltpu.roll(outer[:LANES, :LANES], 0, 1, stride=1, stride_axis=0)
    far = outer[:LANES, LANES:] + outer[LANES:, :LANES]
    far = pltpu.roll(far, 0, 1, stride=1, stride_axis=0)
    first = jnp.sum(jnp.where(keep, near, 0.0), axis=0, keepdims=True)
    second = jnp.sum(jnp.where(keep, far, near), axis=0, keepdims=True)
    return first, second


def pair_kernel(first_s, count_s, flag_ref, times_ref, r_ref, *refs):
    s_refs = refs[:count_s]
    out_ref, scaled, outer, times_buf, r_buf, sems = refs[count_s:]
    length, stations = s_refs[0].shape
    _, windows, group, window_len, _ = r_ref.shape
    chunks = stations // LANES
    count_r = flag_ref.shape[0]

    def fetches(number, to):
        for w in range(windows):
            yield pltpu.make_async_copy(
                r_ref.at[number // group, w, lax.rem(number, group)],
                r_buf.at[to, pl.ds(w * window_len, window_len)],
                sems.at[to, w],
            )
        yield pltpu.make_async_copy(
            times_ref.at[number, pl.ds(first_s, count_s)], times_buf.at[to], sems.at[to, windows]
        )

    for fetch in fetches(0, 0):
        fetch.start()

    def products(r, carry):
        slot = lax.rem(r, 2)

        @pl.when(r + 1 < count_r)
        def _():
            for fetch in fetches(r + 1, 1 - slot):
                fetch.start()

        for fetch in fetches(r, slot):
            fetch.wait()

        for s in range(count_s):
            for c in range(chunks):
                cols = slice(c * LANES, (c + 1) * LANES)
                times = jnp.broadcast_to(times_buf[slot, s, c : c + 1, :], (16, LANES)).astype(jnp.bfloat16)
                times = jnp.concatenate([times] * (length // 16), axis=0)
                scaled[s * length : (s + 1) * length, cols] = s_refs[s][:, cols] * times
        outer[...] = lax.dot_general(scaled[...], r_buf[slot], NT_DIMS, preferred_element_type=jnp.float32)
        for s in range(count_s):
            first, second = antidiagonals(outer[s * length : (s + 1) * length, :])
            out_ref[r, s, 0:1, :] = first
            out_ref[r, s, 1:2, :] = second

        odd = flag_ref[r, first_s]
        for s in range(1, count_s):
            odd = odd | flag_ref[r, first_s + s]

        @pl.when(odd != 0)
        def _():
            for s in range(count_s):
                rows = slice(s * length, (s + 1) * length)
                flag = flag_ref[r, first_s + s]

                @pl.when(flag != 0)
                def _():
                    def one(pair, carry):
                        @pl.when((flag >> pair) & 1 != 0)
                        def _():
                            parts = []
                            for half in range(2):
                                cols = pl.ds(pl.multiple_of((pair * 2 + half) * LANES, LANES), LANES)
                                times = times_buf[slot, s, pl.ds(pair * 2 + half, 1), :]
                                whole = s_refs[s][:, cols].astype(jnp.float32) * jnp.broadcast_to(times, (length, LANES))
                                parts.append((whole - scaled[rows, cols].astype(jnp.float32)).astype(jnp.bfloat16))
                            both = pl.ds(pl.multiple_of(pair * 2 * LANES, 2 * LANES), 2 * LANES)
                            rest = lax.dot_general(
                                jnp.concatenate(parts, axis=1),
                                r_buf[slot, :, both],
                                NT_DIMS,
                                preferred_element_type=jnp.float32,
                            )
                            first, second = antidiagonals(rest)
                            out_ref[r, s, 0:1, :] += first
                            out_ref[r, s, 1:2, :] += second

                        return carry

                    lax.fori_loop(0, chunks // 2, one, 0)

        return carry

    lax.fori_loop(0, count_r, products, 0)


def predict(flags, times, r_shots, s_shots, first_s):
    count_r, count_s = flags.shape[0], len(s_shots)
    length, stations = s_shots[0].shape
    on_chip = pl.BlockSpec(memory_space=pltpu.VMEM)
    return pl.pallas_call(
        functools.partial(pair_kernel, first_s, count_s),
        in_specs=[pl.BlockSpec(memory_space=pltpu.SMEM)]
        + [pl.BlockSpec(memory_space=pltpu.HBM)] * 2
        + [on_chip] * count_s,
        out_specs=on_chip,
        scratch_shapes=[
            pltpu.VMEM((count_s * length, stations), jnp.bfloat16),
            pltpu.VMEM((count_s * length, length), jnp.float32),
            pltpu.VMEM((2, count_s) + times.shape[2:], jnp.float32),
            pltpu.VMEM((2, length, stations), jnp.bfloat16),
            pltpu.SemaphoreType.DMA((2, 5)),
        ],
        out_shape=jax.ShapeDtypeStruct((count_r, count_s, 2, LANES), jnp.float32),
        compiler_params=pltpu.CompilerParams(vmem_limit_bytes=GRANT << 20),
        cost_estimate=pl.CostEstimate(flops=2 * 10**9, bytes_accessed=2**20, transcendentals=0),
        name="pairs",
    )(flags, times, r_shots, *s_shots)


def body(signals, aperture, counts):
    length_win, group, stations = signals.shape
    shots = aperture.shape[1]
    slots = aperture.shape[2]
    z, y, c, x = (lax.axis_index(name) for name in AXES)

    live = jnp.arange(slots, dtype=jnp.int32) < counts[:, :, None]
    lists = jnp.where(live, aperture, -1).reshape(group, 16, 2, 4, slots)
    lists = lax.dynamic_index_in_dim(lists, x, 3, keepdims=False)
    mine = lax.dynamic_index_in_dim(lists, c, 2, keepdims=False)
    theirs = from_offset(lax.dynamic_index_in_dim(lists, 1 - c, 2, keepdims=False), dc=1)

    native = lax.optimization_barrier(jnp.transpose(signals, (1, 0, 2)))
    own = lax.all_to_all(native, "x", 0, 0, tiled=True).reshape(4 * length_win, stations)
    r_shots = lax.all_gather(native, ("c", "x"), axis=0).reshape(2, 4, group, length_win, stations)

    held = {(0, 0): own}
    blocks = []

    def travel(number):
        for offset, (dz, dy), forwarded in ROUNDS[number]:
            held[offset] = from_offset(held[forwarded], dz=dz, dy=dy)

    def meet(number, others):
        names = list(held) if number == 1 else [hop[0] for hop in ROUNDS[number]]
        values = lax.optimization_barrier([held[name] for name in names] + list(others))
        held.update(zip(names, values))
        return values[len(names) :]

    def made_of(first_s, count_s):
        s_shots = [held[offset] for offset in S_OFFSETS[first_s : first_s + count_s]]
        return predict(flags, times, r_shots, s_shots, first_s)

    travel(0)
    lists = jnp.stack([mine, theirs]).reshape(2 * group * 16, slots)
    list_rows, made_rows = row_tables()
    device = ((z * 4 + y) * 2 + c) * 4 + x
    rows = lax.dynamic_index_in_dim(jnp.asarray(list_rows), device, 0, keepdims=False)
    lists = lists.at[rows].get(mode="promise_in_bounds").reshape(2 * group, 16, slots)
    times = station_counts(lists)
    whole = times.astype(jnp.int32).reshape(2 * group, 16, 8, 2 * LANES)
    odd = jnp.max((whole & (whole - 1) != 0).astype(jnp.int32), axis=3)
    flags = jnp.sum(odd << jnp.arange(8, dtype=jnp.int32), axis=2)
    made_row = lax.dynamic_index_in_dim(jnp.asarray(made_rows), device, 0, keepdims=False)
    flags, made_row = meet(0, (flags, made_row))

    travel(1)
    blocks += meet(1, [made_of(0, 4)])
    travel(2)
    blocks += meet(2, [made_of(4, 5)])
    travel(3)
    blocks += meet(3, [made_of(9, 4)])
    blocks.append(made_of(13, 3))
    made = jnp.concatenate(blocks, axis=1).reshape(2 * group * 16, 4 * length_win)

    made = made.at[made_row].get(mode="promise_in_bounds").reshape(2, group, 16, 4, length_win)
    made = jnp.transpose(made, (0, 3, 4, 1, 2)).reshape(8, -1, LANES)
    made = lax.all_to_all(made, ("c", "x"), 0, 0, tiled=True)
    made = made.reshape(2, 4, length_win, group, 16)
    return jnp.transpose(made, (2, 4, 0, 1, 3)).reshape(length_win, shots, group)


def solution(mesh):
    fine = Mesh(np.asarray(mesh.devices).reshape(SIZES), AXES)
    shot = ("z", "y", "c")
    in_specs = (P("x", shot, None), P(shot, None, None), P(shot, None))
    return jax.shard_map(body, mesh=fine, in_specs=in_specs, out_specs=P("x", None, shot), check_vma=False)
```
